32 devices in a mesh: groups: 2 (over y), blk: 4 (over z), heads: 4 (over x, core).
Axes of the slice: x: 2, y: 2, z: 4, core: 2. Of those that a mesh axis runs over, the one named last changes fastest.
Arguments:
- cand_feat: bfloat16 [256, 2048], P(('groups', 'blk')), parts along dimension 0, may hold values from -6 to 6
- cand_counts: int32 [4], P('groups'), parts along dimension 0, may hold values from 1 to 102, 128 in all
- proj_weight: bfloat16 [2, 2048, 2048], P(None, None, 'heads'), may hold values from -0.125 to 0.125
- norm_gain: bfloat16 [2048], P('heads'), may hold values from 0.25 to 1.75
- hist_kv: bfloat16 [2, 16384, 2048], P(None, ('groups', 'blk'), 'heads'), parts along dimension 1, may hold values from -6 to 6
- hist_lens: int32 [4], P('groups'), parts along dimension 0, may hold values from 1 to 6144, 8192 in all
- hist_mask: int32 [16384], P(('groups', 'blk')), parts along dimension 0, may hold values 0 or 1
- out_cot: bfloat16 [256, 2048], P(('groups', 'blk'), 'heads'), parts along dimension 0, may hold values from -6 to 6
- owner: int32 [256, 1], P(('groups', 'blk')), parts along dimension 0, may hold values from 0 to 3; in each aligned block of 32 rows (0 to 31, 32 to 63, ...) at most 24 rows name the same one
- item_row: int32 [256], P(('groups', 'blk')), parts along dimension 0, may hold values from 0 to 47
Outputs:
- attended: bfloat16 [256, 2048], P(('groups', 'blk'), 'heads'), parts along dimension 0
- item_grad: float32 [384, 2048], P(('groups', 'blk'), 'heads'), parts along dimension 0
The draws below stay inside these ranges and needn't reach their ends.
There are 2 independent parts, one for each index of `groups`. The reference program is written for one: setup_inputs(seed, part) draws one part's arguments, and reference() takes and returns one part's arrays. A program takes and returns all parts, laid end to end along the dimension named above; an argument that names none is the same for every part. Nothing has to cross between parts.
Inputs may be any that keep to these rules, and one draw needn't show every extreme that they name: `cand_counts`: the counts sum to 128; candidates are laid out user after user. `hist_lens`: the lengths sum to 8192; events are laid out user after user. Among the candidates of one device, at most 24 name the same owner.
All inputs are finite; a program needn't handle non-finite values. No bound on the sum of `hist_mask` on one device may be relied on, other than what follows from the above.
Results may differ from the reference program's by a relative error of at most 0.006.
Values may be sent and summed in bfloat16 or wider, within the bound.
No kernel may reach another device: no remote copies, remote signals or barrier semaphores. Data moves between devices by JAX's collectives and lax.ppermute only.
A program may use at most 64 MiB of HBM per device.

```python
import math
import jax
import jax.numpy as jnp
import numpy as np
from jax import lax

D = 2048
HEADS = 16
HD = 128
USERS = 2
CAND_DEV = 32
ITEMS_DEV = 48
HIST = 8192
CAND = 128
OWN_CAP = 24
N_BLK = 4


def touch_ends(values, stream_key, smallest, top_value):
    dims = values.shape
    place = [jax.random.randint(jax.random.fold_in(stream_key, axis), (), 0, dims[axis]) for axis in range(len(dims))]
    values = values.at[tuple(place)].set(smallest)
    longest = dims.index(max(dims))
    place[longest] = (place[longest] + 1) % dims[longest]
    return values.at[tuple(place)].set(top_value)


def steps_of(own_key, extent, pieces, low, high):
    factor_of, own = 1.0, jax.random.fold_in(own_key, 6)
    for axis_at, parts in pieces:
        steps = jnp.exp(jax.random.uniform(jax.random.fold_in(own, axis_at), (parts,), jnp.float32, low / len(pieces), high / len(pieces)))
        factor_of = factor_of * jnp.repeat(steps, extent[axis_at] // parts).reshape([-1 if axis == axis_at else 1 for axis in range(len(extent))])
    return factor_of


def length_profile(number_of, total, bound, skew):
    loads = [(1 << 20) // math.isqrt(rank ** skew) + 1 for rank in range(2, number_of + 1)]
    rest, given = total - bound - (number_of - 1), [1] * (number_of - 1)
    while rest > 0:
        movable = [i for i in range(number_of - 1) if given[i] < bound]
        mass, remaining = sum([loads[i] for i in movable]), rest
        for i in movable:
            addition = min(bound - given[i], max(1, remaining * loads[i] // mass), rest)
            given[i] = given[i] + addition
            rest = rest - addition
    return np.array([bound] + given)


def uneven_parts(key, amount, total, bound, lean):
    if amount == 2:
        one = jax.random.randint(key, (), max(1, total - bound), min(bound, total - 1) + 1)
        return jnp.stack([one, total - one])
    tallies = jnp.asarray(length_profile(amount, total, bound, lean), jnp.int32)
    pairs = (amount - 1) // 2
    giver, receiver = tallies[1:1 + 2 * pairs:2], tallies[2:2 + 2 * pairs:2]
    margin = jnp.minimum(giver - 1, bound - receiver)
    passed = jax.random.randint(jax.random.fold_in(key, 1), (pairs,), 0, 1 << 20) % (margin + 1)
    tallies = tallies.at[1:1 + 2 * pairs:2].set(giver - passed).at[2:2 + 2 * pairs:2].set(receiver + passed)
    return tallies[jax.random.permutation(jax.random.fold_in(key, 2), amount)]


def routed_block(stream_key, own, number, rows, amount, top, bound, slope):
    ranking = jax.random.permutation(stream_key, amount)
    heavy_load, common = portions_of(amount, rows * top, bound, slope, True), portions_of(amount, rows * top, bound, slope, False)
    places = jnp.arange(amount)

    def named(tallies, turn):
        used = int((tallies > 0).sum())
        fixed = max(1, used // 4)
        passed = fixed + (places - fixed + turn * (used - fixed)) % max(1, amount - fixed)
        return jnp.zeros((amount,), jnp.int32).at[ranking[jnp.where(places < fixed, places, passed)]].set(jnp.asarray(tallies, jnp.int32))

    tallies = jnp.where(number % 4 == 0, named(heavy_load, number // 4), named(common, number - number // 4 - 1))
    mixed = jax.random.permutation(jax.random.fold_in(own, 3), amount)
    donor, sink = mixed[0:amount // 2 * 2:2], mixed[1:amount // 2 * 2:2]
    margin = jnp.minimum(tallies[donor] - 1, bound - tallies[sink]) // 2
    margin = jnp.where((donor == ranking[0]) | (sink == ranking[0]) | (tallies[sink] == 0), 0, jnp.maximum(margin, 0))
    passed = jax.random.randint(jax.random.fold_in(own, 4), (amount // 2,), 0, 1 << 20) % (margin + 1)
    tallies = tallies.at[donor].add(-passed).at[sink].add(passed)
    items = jnp.searchsorted(jnp.cumsum(tallies), jnp.arange(rows * top), side="right").astype(jnp.int32)
    grid = items.reshape(top, rows).T
    grid = grid[jax.random.permutation(jax.random.fold_in(own, 1), rows)]
    turn = jax.random.randint(jax.random.fold_in(own, 2), (rows, 1), 0, top)
    return jnp.take_along_axis(grid, (jnp.arange(top)[None, :] + turn) % top, axis=1)


def portions_of(number_of, total, most, slope, full):
    portions = [(1 << 20) // math.isqrt(rank ** slope) + 1 for rank in range(1, number_of + 1)]
    largest = most if full else min(most, max(-(-total // number_of), total * portions[0] // sum(portions)))
    least = 1 if total - largest >= number_of - 1 else 0
    holding, surplus = [largest] + [least] * (number_of - 1), total - largest - least * (number_of - 1)
    while surplus > 0:
        candidates = [i for i in range(1, number_of) if holding[i] < largest] or [i for i in range(1, number_of) if holding[i] < most]
        whole, remaining = sum([portions[i] for i in candidates]), surplus
        for i in candidates:
            extra = min(most - holding[i], max(1, remaining * portions[i] // whole), surplus)
            holding[i] = holding[i] + extra
            surplus = surplus - extra
    return np.array(holding)


def gaussian(key, shape, deviation, most, cuts=(), kind=jnp.bfloat16):
    gain = steps_of(key, shape, cuts, -0.22, 0.18) if cuts else 1.0
    result = jax.random.normal(key, shape, jnp.float32) * deviation * gain
    return jnp.minimum(jnp.maximum(result, -most), most).astype(kind)


def setup_inputs(seed: int = 0, part: int = 0) -> dict:
    seeds = jax.random.split(jax.random.key(seed), 11)
    part_splits = jax.random.split(jax.random.fold_in(seeds[10], part), 11)
    cand_feat = gaussian(part_splits[0], (CAND, D), 1.0, 6.0, ((0, 4),))
    cand_counts = uneven_parts(part_splits[1], USERS, CAND, CAND * 4 // 5, 2).astype(jnp.int32)
    proj_weight = gaussian(seeds[2], (2, D, D), D ** -0.5, 0.125, ((2, 4),))
    norm_gain = jnp.clip(1.0 + 0.15 * jax.random.normal(seeds[3], (D,), jnp.float32), 0.25, 1.75).astype(jnp.bfloat16)
    hist_kv = gaussian(part_splits[4], (2, HIST, D), 1.0, 6.0, ((1, 4), (2, 4)))
    hist_lens = uneven_parts(part_splits[5], USERS, HIST, HIST * 3 // 4, 2).astype(jnp.int32)
    hist_mask = touch_ends((jax.random.randint(part_splits[6], (HIST,), 0, 8) < 7).astype(jnp.int32), jax.random.fold_in(part_splits[6], 1), 0, 1)
    out_cot = gaussian(part_splits[7], (CAND, D), 1.0, 6.0, ((0, 4), (1, 4)))
    owner_keys = jax.random.split(jax.random.fold_in(part_splits[8], 1), CAND // CAND_DEV)
    owner_turns = jax.random.permutation(jax.random.fold_in(part_splits[8], 3), CAND // CAND_DEV)
    owner = jax.vmap(lambda own, number: routed_block(jax.random.fold_in(part_splits[8], 2), own, number, CAND_DEV, N_BLK, 1, OWN_CAP, 2))(owner_keys, owner_turns).reshape((CAND, 1))
    item_row = touch_ends(jax.random.randint(part_splits[9], (CAND,), 0, ITEMS_DEV), jax.random.fold_in(part_splits[9], 1), 0, ITEMS_DEV - 1).astype(jnp.int32)
    return dict(cand_feat=cand_feat, cand_counts=cand_counts, proj_weight=proj_weight, norm_gain=norm_gain, hist_kv=hist_kv, hist_lens=hist_lens, hist_mask=hist_mask, out_cot=out_cot, owner=owner, item_row=item_row)


NORM_EPS = 1e-05

def silu_grad(values):
    sigmoid = jax.nn.sigmoid(values)
    return sigmoid * (1.0 + values * (1.0 - sigmoid))

def segment_user(counts, positions):
    segment_ends = jnp.cumsum(counts)
    return lax.optimization_barrier(jnp.sum((positions[:, None] >= segment_ends[None, :]).astype(jnp.int32), axis=1))

def reference(cand_feat, cand_counts, proj_weight, norm_gain, hist_kv, hist_lens, hist_mask, out_cot, owner, item_row):
    cand_total = cand_feat.shape[0]
    hist_total = hist_kv.shape[1]
    score_scale = HD ** (-0.5)
    query_pre = jnp.dot(cand_feat, proj_weight[0], preferred_element_type=jnp.float32)
    up_pre = jnp.dot(cand_feat, proj_weight[1], preferred_element_type=jnp.float32)
    queries = jax.nn.silu(query_pre).astype(jnp.bfloat16)
    gate_act = jax.nn.silu(up_pre)
    cand_user = segment_user(cand_counts, jnp.arange(cand_total, dtype=jnp.int32))
    hist_user = segment_user(hist_lens, jnp.arange(hist_total, dtype=jnp.int32))
    live = hist_mask > 0

    def keep_mask():
        return ((cand_user[:, None] == hist_user[None, :]) & live[None, :]).astype(jnp.float32)
    query_heads = jnp.transpose(queries.reshape(cand_total, HEADS, HD), (1, 0, 2))
    key_heads = jnp.transpose(hist_kv[0].reshape(hist_total, HEADS, HD), (1, 0, 2))
    value_heads = jnp.transpose(hist_kv[1].reshape(hist_total, HEADS, HD), (1, 0, 2))

    def head_forward(operands):
        query_h, key_h, value_h = operands
        scores = jnp.dot(query_h, key_h.T, preferred_element_type=jnp.float32) * score_scale
        attention = (jax.nn.silu(scores) * keep_mask()).astype(jnp.bfloat16)
        return jnp.dot(attention, value_h, preferred_element_type=jnp.float32)
    attended_sum = lax.map(head_forward, (query_heads, key_heads, value_heads))
    mean_square = lax.optimization_barrier(jnp.mean(attended_sum * attended_sum, axis=-1, keepdims=True))
    inv_rms = lax.rsqrt(mean_square + NORM_EPS)
    normed = attended_sum * inv_rms
    gain_heads = norm_gain.astype(jnp.float32).reshape(HEADS, 1, HD)
    gate_heads = jnp.transpose(gate_act.reshape(cand_total, HEADS, HD), (1, 0, 2))
    attended = jnp.transpose(normed * gain_heads * gate_heads, (1, 0, 2)).reshape(cand_total, HEADS * HD).astype(jnp.bfloat16)
    cot_heads = jnp.transpose(out_cot.astype(jnp.float32).reshape(cand_total, HEADS, HD), (1, 0, 2))
    gate_grad = cot_heads * normed * gain_heads
    up_grad = (jnp.transpose(gate_grad, (1, 0, 2)).reshape(cand_total, HEADS * HD) * silu_grad(up_pre)).astype(jnp.bfloat16)
    normed_grad = cot_heads * gate_heads * gain_heads
    av_grad = (inv_rms * (normed_grad - normed * lax.optimization_barrier(jnp.mean(normed_grad * normed, axis=-1, keepdims=True)))).astype(jnp.bfloat16)

    def head_backward(operands):
        query_h, grad_h, key_h, value_h = operands
        scores = jnp.dot(query_h, key_h.T, preferred_element_type=jnp.float32) * score_scale
        along = jnp.dot(grad_h, value_h.T, preferred_element_type=jnp.float32)
        score_grad = (silu_grad(scores) * keep_mask() * along).astype(jnp.bfloat16)
        return jnp.dot(score_grad, key_h, preferred_element_type=jnp.float32)
    query_sum = lax.map(head_backward, (query_heads, av_grad, key_heads, value_heads))
    query_grad = jnp.transpose(query_sum, (1, 0, 2)).reshape(cand_total, HEADS * HD) * score_scale
    query_pre_grad = (query_grad * silu_grad(query_pre)).astype(jnp.bfloat16)
    feature_grad = jnp.dot(query_pre_grad, proj_weight[0].T, preferred_element_type=jnp.float32) + jnp.dot(up_grad, proj_weight[1].T, preferred_element_type=jnp.float32)
    table_row = (owner[:, 0] * ITEMS_DEV + item_row).astype(jnp.int32)
    item_grad = jax.ops.segment_sum(feature_grad, table_row, num_segments=ITEMS_DEV * N_BLK)
    return (attended, item_grad)
```

```python
import functools

import jax
import jax.numpy as jnp
from jax import lax
from jax.experimental import pallas as pl
from jax.experimental.pallas import tpu as pltpu
from jax.sharding import PartitionSpec as P

HD = 128
ITEMS_DEV = 48
NORM_EPS = 1e-05
SCALE = HD ** (-0.5)
IDX_LANES = 128
DIRECT = 4

BF = jnp.bfloat16
F32 = jnp.float32
VMEM = pltpu.MemorySpace.VMEM
SMEM = pltpu.MemorySpace.SMEM


def silu(v):
    half = v * 0.5
    return half * jnp.tanh(half) + half


def silu_grad(v):
    half = v * 0.5
    t = jnp.tanh(half)
    return 0.5 * (1.0 + t + half * (1.0 - t * t))


def dot_nt(a, b):
    return lax.dot_general(a, b, (((1,), (1,)), ((), ())), preferred_element_type=F32)


def dot_nn(a, b):
    return lax.dot_general(a, b, (((1,), (0,)), ((), ())), preferred_element_type=F32)


def dot_tn(a, b):
    return lax.dot_general(a, b, (((0,), (0,)), ((), ())), preferred_element_type=F32)


def vmem_full(shape):
    return pl.BlockSpec(shape, lambda *_: (0,) * len(shape))


def smem_spec():
    return pl.BlockSpec(memory_space=SMEM)


def slot_order(axis):
    return lax.axis_index(axis) ^ jnp.arange(lax.axis_size(axis), dtype=jnp.int32)


def send(x, axis, m):
    return lax.ppermute(x, axis, [(j, j ^ m) for j in range(lax.axis_size(axis))])


def gather_slots(x, axis):
    n = lax.axis_size(axis)
    if n <= DIRECT:
        return [x] + [send(x, axis, m) for m in range(1, n)]
    whole = lax.all_gather(x, axis)[slot_order(axis)]
    return [whole[m] for m in range(n)]


def scatter_slots(tiles, axis):
    n = lax.axis_size(axis)
    if n <= DIRECT:
        return [tiles[0]] + [send(tiles[m], axis, m) for m in range(1, n)]
    stacked = jnp.stack([t.astype(F32) for t in tiles])[slot_order(axis)]
    return [lax.psum_scatter(stacked, axis, scatter_dimension=0, tiled=False)]


def proj_query_kernel(x_ref, w_ref, out_ref, acc_ref):
    k = pl.program_id(0)

    @pl.when(k == 0)
    def _():
        acc_ref[...] = jnp.zeros_like(acc_ref)

    acc_ref[...] += dot_nn(x_ref[...], w_ref[0])

    @pl.when(k == pl.num_programs(0) - 1)
    def _():
        out_ref[...] = acc_ref[...].astype(BF)


def proj_up_kernel(x_ref, w_ref, cot_ref, owner_ref, row_ref, pack_ref, up_ref):
    k = pl.program_id(0)
    cols = up_ref.shape[1]

    @pl.when(k == 0)
    def _():
        up_ref[...] = jnp.zeros_like(up_ref)

    up_ref[...] += dot_nn(x_ref[...], w_ref[0])

    @pl.when(k == pl.num_programs(0) - 1)
    def _():
        rows = up_ref.shape[0]
        pack_ref[:, :cols] = cot_ref[...]
        pack_ref[:, cols : 2 * cols] = up_ref[...].astype(BF)
        lane = lax.broadcasted_iota(jnp.int32, (rows, IDX_LANES), 1)
        idx = jnp.where(lane == 0, owner_ref[...], row_ref[...]).astype(F32)
        pack_ref[:, 2 * cols :] = idx.astype(BF)


def user_of(pos, counts_ref):
    user = jnp.zeros_like(pos)
    end = jnp.int32(0)
    for u in range(counts_ref.shape[0]):
        end = end + counts_ref[u]
        user = user + (pos >= end).astype(jnp.int32)
    return user


def keep_mask(slots, rows, width, first_key, me, counts_ref, lens_ref, live):
    cand = jnp.concatenate(
        [
            lax.broadcasted_iota(jnp.int32, (rows, 1), 0) + (me ^ m) * rows
            for m in range(slots)
        ],
        axis=0,
    )
    key = lax.broadcasted_iota(jnp.int32, (1, width), 1) + first_key
    key_user = jnp.where(live > 0, user_of(key, lens_ref), -1)
    return user_of(cand, counts_ref) == key_user


def forward_kernel(slots, me_ref, counts_ref, lens_ref, live_ref, *refs):
    pre_refs = refs[:slots]
    key_ref, value_ref, sum_ref, low_ref, query_ref = refs[slots:]
    k = pl.program_id(0)
    rows = pre_refs[0].shape[0]
    cols = sum_ref.shape[1]
    width = key_ref.shape[1]
    me = me_ref[0]

    @pl.when(k == 0)
    def _():
        sum_ref[...] = jnp.zeros_like(sum_ref)
        for m in range(slots):
            query_ref[m * rows : (m + 1) * rows, :] = silu(pre_refs[m][...].astype(F32)).astype(BF)

    first = (me * pl.num_programs(0) + k) * width
    keep = keep_mask(slots, rows, width, first, me, counts_ref, lens_ref, live_ref[...])
    for h in range(cols // HD):
        at = slice(h * HD, (h + 1) * HD)
        half = dot_nt(query_ref[:, at], key_ref[0, :, at]) * (0.5 * SCALE)
        att = jnp.where(keep, half * jnp.tanh(half) + half, 0.0).astype(BF)
        sum_ref[:, at] += dot_nn(att, value_ref[0, :, at])

    @pl.when(k == pl.num_programs(0) - 1)
    def _():
        low_ref[...] = sum_ref[...].astype(BF)


def slope_kernel(slots, rows, me_ref, counts_ref, lens_ref, live_ref, query_ref, key_ref, out_ref):
    k = pl.program_id(0)
    width = key_ref.shape[1]
    me = me_ref[0]
    first = (me * pl.num_programs(0) + k) * width
    keep = keep_mask(slots, rows, width, first, me, counts_ref, lens_ref, live_ref[...])
    for h in range(query_ref.shape[1] // HD):
        at = slice(h * HD, (h + 1) * HD)
        half = dot_nt(query_ref[:, at], key_ref[0, :, at]) * (0.5 * SCALE)
        t = jnp.tanh(half)
        slope = 1.0 + t + half * (1.0 - t * t)
        out_ref[h] = jnp.where(keep, slope, 0.0).astype(BF)


def backward_kernel(slots, *refs):
    me_ref, gain_ref, up_ref, sum_ref = refs[:4]
    refs = refs[4:]
    got = refs[: len(refs) - 9 - 3 * slots]
    refs = refs[len(got) :]
    pre_refs, pack_refs = refs[:slots], refs[slots : 2 * slots]
    refs = refs[2 * slots :]
    slope_ref, key_ref, value_ref, att_ref, upt_ref = refs[:5]
    tile_refs = refs[5 : 5 + slots]
    acc_ref, grad_ref, ug_ref, tot_ref = refs[5 + slots :]
    k = pl.program_id(0)
    rows, cols = up_ref.shape
    heads = cols // HD
    me = me_ref[0]

    @pl.when(k == 0)
    def _():
        acc_ref[...] = jnp.zeros_like(acc_ref)
        for s in range(slots):
            block = slice(s * rows, (s + 1) * rows)
            total = sum_ref[block, :]
            for m in range(1, len(got) + 1):
                other = s ^ m
                total = total + got[m - 1][other * rows : (other + 1) * rows, :].astype(F32)
            for h in range(heads):
                at = slice(h * HD, (h + 1) * HD)
                part = total[:, at]
                inv = lax.rsqrt(jnp.mean(part * part, axis=-1, keepdims=True) + NORM_EPS)
                normed = part * inv
                gain = gain_ref[:, at].astype(F32)
                if s == 0:
                    up = up_ref[:, at]
                else:
                    up = pack_refs[s][:, cols + h * HD : cols + (h + 1) * HD].astype(F32)
                cot = pack_refs[s][:, at].astype(F32)
                gate = silu(up)
                if s == 0:
                    att_ref[:, at] = (normed * gain * gate).astype(BF)
                ug_ref[block, at] = (cot * normed * gain * silu_grad(up)).astype(BF)
                ngr = cot * gate * gain
                mean = jnp.mean(ngr * normed, axis=-1, keepdims=True)
                grad_ref[block, at] = (inv * (ngr - normed * mean)).astype(BF)

    for h in range(heads):
        at = slice(h * HD, (h + 1) * HD)
        along = dot_nt(grad_ref[:, at], value_ref[0, :, at])
        score_grad = (slope_ref[h].astype(F32) * along).astype(BF)
        acc_ref[:, at] += dot_nn(score_grad, key_ref[0, :, at])

    @pl.when(k == pl.num_programs(0) - 1)
    def _():
        for s in range(slots):
            block = slice(s * rows, (s + 1) * rows)
            slope = silu_grad(pre_refs[s][...].astype(F32))
            grad_ref[block, :] = (acc_ref[block, :] * (0.5 * SCALE) * slope).astype(BF)
        own = jnp.concatenate([r[:, 2 * cols : 2 * cols + 1] for r in pack_refs], axis=0).astype(F32)
        row = jnp.concatenate([r[:, 2 * cols + 1 : 2 * cols + 2] for r in pack_refs], axis=0).astype(F32)
        at_row = lax.broadcasted_iota(jnp.int32, (slots * rows, ITEMS_DEV), 1).astype(F32)
        here = row == at_row
        for m in range(slots):
            mine = own == (me ^ m).astype(F32)
            pick = jnp.where(here & mine, 1.0, 0.0).astype(BF)
            tile_refs[m][...] = dot_tn(pick, grad_ref[...]).astype(tile_refs[m].dtype)
            if m == 0:
                upt_ref[...] = dot_tn(pick, ug_ref[...]).astype(BF)


def weight_kernel(slots, terms, me_ref, upt_ref, *refs):
    term_refs, w_ref = refs[:terms], refs[terms]
    out_refs = refs[terms + 1 : terms + 1 + slots]
    sum_ref = refs[terms + 1 + slots]
    k = pl.program_id(0)

    @pl.when(k == 0)
    def _():
        total = term_refs[0][...]
        for r in term_refs[1:]:
            total = total + r[...].astype(F32)
        sum_ref[...] = total.astype(BF)

    part = dot_nt(sum_ref[...], w_ref[0]) + dot_nt(upt_ref[...], w_ref[1])
    for m in range(slots):

        @pl.when(k == m)
        def _():
            out_refs[m][...] = part.astype(out_refs[m].dtype)


def body(
    cand_feat,
    cand_counts,
    proj_weight,
    norm_gain,
    hist_kv,
    hist_lens,
    hist_mask,
    out_cot,
    owner,
    item_row,
):
    rows, depth = cand_feat.shape
    slots = lax.axis_size("blk")
    wide = lax.axis_size("heads")
    cols = proj_weight.shape[2]
    heads = cols // HD
    cands = rows * slots
    keys = hist_kv.shape[1]
    me = lax.axis_index("blk").astype(jnp.int32).reshape(1)
    head_me = lax.axis_index("heads").astype(jnp.int32).reshape(1)
    live = hist_mask.reshape(1, keys)
    kstep = min(512, depth)
    width = min(512, keys)
    chunks = keys // width
    sds = jax.ShapeDtypeStruct

    x_spec = pl.BlockSpec((rows, kstep), lambda k: (0, k))
    pre = pl.pallas_call(
        proj_query_kernel,
        grid=(depth // kstep,),
        in_specs=[x_spec, pl.BlockSpec((1, kstep, cols), lambda k: (0, k, 0))],
        out_specs=vmem_full((rows, cols)),
        out_shape=sds((rows, cols), BF),
        scratch_shapes=[pltpu.VMEM((rows, cols), F32)],
        name="proj_query",
    )(cand_feat, proj_weight)
    pre_slots = gather_slots(pre, "blk")

    pack_cols = 2 * cols + IDX_LANES
    pack, up = pl.pallas_call(
        proj_up_kernel,
        grid=(depth // kstep,),
        in_specs=[
            x_spec,
            pl.BlockSpec((1, kstep, cols), lambda k: (1, k, 0)),
            vmem_full((rows, cols)),
            vmem_full((rows, 1)),
            vmem_full((rows, 1)),
        ],
        out_specs=[vmem_full((rows, pack_cols)), vmem_full((rows, cols))],
        out_shape=[sds((rows, pack_cols), BF), sds((rows, cols), F32)],
        name="proj_up",
    )(cand_feat, proj_weight, out_cot, owner, item_row.reshape(rows, 1))
    pack_slots = gather_slots(pack, "blk")

    key_spec = pl.BlockSpec((1, width, cols), lambda k: (0, k, 0))
    value_spec = pl.BlockSpec((1, width, cols), lambda k: (1, k, 0))
    live_spec = pl.BlockSpec((1, width), lambda k: (0, k))
    block = vmem_full((rows, cols))
    every = vmem_full((cands, cols))
    sums, low, queries = pl.pallas_call(
        functools.partial(forward_kernel, slots),
        grid=(chunks,),
        in_specs=[smem_spec()] * 3 + [live_spec] + [block] * slots + [key_spec, value_spec],
        out_specs=[every, every, every],
        out_shape=[sds((cands, cols), F32), sds((cands, cols), BF), sds((cands, cols), BF)],
        name="attend",
    )(me, cand_counts, hist_lens, live, *pre_slots, hist_kv, hist_kv)

    if slots <= DIRECT:
        got = [send(low, "blk", m) for m in range(1, slots)]
    else:
        order = slot_order("blk")
        whole = lax.psum(sums.reshape(slots, rows, cols)[order], "blk")
        sums, got = whole[order].reshape(cands, cols), []

    slope = pl.pallas_call(
        functools.partial(slope_kernel, slots, rows),
        grid=(chunks,),
        in_specs=[smem_spec()] * 3 + [live_spec, every, key_spec],
        out_specs=pl.BlockSpec((heads, cands, width), lambda k: (0, 0, k)),
        out_shape=sds((heads, cands, keys), BF),
        name="slope",
    )(me, cand_counts, hist_lens, live, queries, hist_kv)

    tile = vmem_full((ITEMS_DEV, cols))
    outs = pl.pallas_call(
        functools.partial(backward_kernel, slots),
        grid=(chunks,),
        in_specs=[smem_spec(), vmem_full((1, cols)), block, every]
        + [every] * len(got)
        + [block] * slots
        + [vmem_full((rows, pack_cols))] * slots
        + [pl.BlockSpec((heads, cands, width), lambda k: (0, 0, k)), key_spec, value_spec],
        out_specs=[block, tile] + [tile] * slots,
        out_shape=[sds((rows, cols), BF), sds((ITEMS_DEV, cols), BF), sds((ITEMS_DEV, cols), F32)]
        + [sds((ITEMS_DEV, cols), BF)] * (slots - 1),
        scratch_shapes=[
            pltpu.VMEM((cands, cols), F32),
            pltpu.VMEM((cands, cols), BF),
            pltpu.VMEM((cands, cols), BF),
            pltpu.VMEM((8, 128), F32),
        ],
        name="attend_grad",
    )(
        me,
        norm_gain.reshape(1, cols),
        up,
        sums,
        *got,
        *pre_slots,
        *pack_slots,
        slope,
        hist_kv,
        hist_kv,
    )
    attended, up_table = outs[0], outs[1]
    terms = scatter_slots(list(outs[2:]), "blk")

    out_cols = depth // wide
    parts = pl.pallas_call(
        functools.partial(weight_kernel, wide, len(terms)),
        grid_spec=pltpu.PrefetchScalarGridSpec(
            num_scalar_prefetch=1,
            grid=(wide,),
            in_specs=[tile] * (1 + len(terms))
            + [pl.BlockSpec((2, out_cols, cols), lambda k, at: (0, at[0] ^ k, 0))],
            out_specs=[vmem_full((ITEMS_DEV, out_cols))] * wide,
            scratch_shapes=[pltpu.VMEM((ITEMS_DEV, cols), BF)],
        ),
        out_shape=[sds((ITEMS_DEV, out_cols), F32)]
        + [sds((ITEMS_DEV, out_cols), BF)] * (wide - 1),
        name="weight_grad",
    )(head_me, up_table, *terms, proj_weight)
    ends = scatter_slots(list(parts), "heads")
    item_grad = ends[0]
    for e in ends[1:]:
        item_grad = item_grad + e.astype(F32)
    return (attended, item_grad)


def solution(mesh):
    return jax.shard_map(
        body,
        mesh=mesh,
        in_specs=(
            P(("groups", "blk"), None),
            P("groups"),
            P(None, None, "heads"),
            P("heads"),
            P(None, ("groups", "blk"), "heads"),
            P("groups"),
            P(("groups", "blk")),
            P(("groups", "blk"), "heads"),
            P(("groups", "blk"), None),
            P(("groups", "blk")),
        ),
        out_specs=(P(("groups", "blk"), "heads"), P(("groups", "blk"), "heads")),
        check_vma=False,
    )
```

```python
import functools

import jax
import jax.numpy as jnp
from jax import lax
from jax.experimental import pallas as pl
from jax.experimental.pallas import tpu as pltpu
from jax.sharding import PartitionSpec as P

HD = 128
ITEMS_DEV = 48
NORM_EPS = 1e-05
SCALE = HD ** (-0.5)
IDX_LANES = 128
DIRECT = 4

BF = jnp.bfloat16
F32 = jnp.float32
VMEM = pltpu.MemorySpace.VMEM
SMEM = pltpu.MemorySpace.SMEM


def silu(v):
    half = v * 0.5
    return half * jnp.tanh(half) + half


def silu_grad(v):
    half = v * 0.5
    t = jnp.tanh(half)
    return 0.5 * (1.0 + t + half * (1.0 - t * t))


def dot_nt(a, b):
    return lax.dot_general(a, b, (((1,), (1,)), ((), ())), preferred_element_type=F32)


def dot_nn(a, b):
    return lax.dot_general(a, b, (((1,), (0,)), ((), ())), preferred_element_type=F32)


def dot_tn(a, b):
    return lax.dot_general(a, b, (((0,), (0,)), ((), ())), preferred_element_type=F32)


def vmem_full(shape):
    return pl.BlockSpec(shape, lambda *_: (0,) * len(shape))


def smem_spec():
    return pl.BlockSpec(memory_space=SMEM)


def slot_order(axis):
    return lax.axis_index(axis) ^ jnp.arange(lax.axis_size(axis), dtype=jnp.int32)


def send(x, axis, m):
    return lax.ppermute(x, axis, [(j, j ^ m) for j in range(lax.axis_size(axis))])


def gather_slots(x, axis):
    n = lax.axis_size(axis)
    if n <= DIRECT:
        return [x] + [send(x, axis, m) for m in range(1, n)]
    whole = lax.all_gather(x, axis)[slot_order(axis)]
    return [whole[m] for m in range(n)]


def scatter_slots(tiles, axis):
    n = lax.axis_size(axis)
    if n <= DIRECT:
        return [tiles[0]] + [send(tiles[m], axis, m) for m in range(1, n)]
    stacked = jnp.stack([t.astype(F32) for t in tiles])[slot_order(axis)]
    return [lax.psum_scatter(stacked, axis, scatter_dimension=0, tiled=False)]


def proj_query_kernel(x_ref, w_ref, query_ref, pre_ref):
    k = pl.program_id(0)

    @pl.when(k == 0)
    def _():
        pre_ref[...] = jnp.zeros_like(pre_ref)

    pre_ref[...] += dot_nn(x_ref[...], w_ref[0])

    @pl.when(k == pl.num_programs(0) - 1)
    def _():
        query_ref[...] = silu(pre_ref[...]).astype(BF)


def proj_up_kernel(x_ref, w_ref, up_ref):
    k = pl.program_id(0)

    @pl.when(k == 0)
    def _():
        up_ref[...] = jnp.zeros_like(up_ref)

    up_ref[...] += dot_nn(x_ref[...], w_ref[0])


def user_of(pos, counts_ref):
    user = jnp.zeros_like(pos)
    end = jnp.int32(0)
    for u in range(counts_ref.shape[0]):
        end = end + counts_ref[u]
        user = user + (pos >= end).astype(jnp.int32)
    return user


def keep_mask(slots, rows, width, first_key, me, counts_ref, lens_ref, live):
    cand = jnp.concatenate(
        [
            lax.broadcasted_iota(jnp.int32, (rows, 1), 0) + (me ^ m) * rows
            for m in range(slots)
        ],
        axis=0,
    )
    key = lax.broadcasted_iota(jnp.int32, (1, width), 1) + first_key
    key_user = jnp.where(live > 0, user_of(key, lens_ref), -1)
    return user_of(cand, counts_ref) == key_user


def forward_kernel(slots, me_ref, counts_ref, lens_ref, live_ref, pre_ref, idx_ref, *refs):
    got_refs = refs[:slots]
    key_ref, value_ref, pack_ref, query_ref = refs[slots : slots + 4]
    tile_refs = refs[slots + 4 : 2 * slots + 4]
    sum_ref = refs[2 * slots + 4]
    k = pl.program_id(0)
    rows, cols = pre_ref.shape
    width = key_ref.shape[1]
    me = me_ref[0]

    @pl.when(k == 0)
    def _():
        sum_ref[...] = jnp.zeros_like(sum_ref)
        pack_ref[:, :cols] = silu_grad(pre_ref[...]).astype(BF)
        pack_ref[:, cols:] = idx_ref[...]
        for m in range(slots):
            query_ref[m * rows : (m + 1) * rows, :] = got_refs[m][...]

    first = (me * pl.num_programs(0) + k) * width
    keep = keep_mask(slots, rows, width, first, me, counts_ref, lens_ref, live_ref[...])
    for h in range(cols // HD):
        at = slice(h * HD, (h + 1) * HD)
        half = dot_nt(query_ref[:, at], key_ref[0, :, at]) * (0.5 * SCALE)
        att = jnp.where(keep, half * jnp.tanh(half) + half, 0.0).astype(BF)
        sum_ref[:, at] += dot_nn(att, value_ref[0, :, at])

    @pl.when(k == pl.num_programs(0) - 1)
    def _():
        for m in range(slots):
            tile_refs[m][...] = sum_ref[m * rows : (m + 1) * rows, :].astype(tile_refs[m].dtype)


def norm_kernel(terms, *refs):
    term_refs = refs[:terms]
    up_ref, cot_ref, gain_ref, att_ref, out_ref = refs[terms:]
    cols = up_ref.shape[1]
    for h in range(cols // HD):
        at = slice(h * HD, (h + 1) * HD)
        total = term_refs[0][:, at]
        for r in term_refs[1:]:
            total = total + r[:, at].astype(F32)
        inv = lax.rsqrt(jnp.mean(total * total, axis=-1, keepdims=True) + NORM_EPS)
        normed = total * inv
        gain = gain_ref[:, at].astype(F32)
        up = up_ref[:, at]
        cot = cot_ref[:, at].astype(F32)
        gate = silu(up)
        att_ref[:, at] = (normed * gain * gate).astype(BF)
        ngr = cot * gate * gain
        mean = jnp.mean(ngr * normed, axis=-1, keepdims=True)
        out_ref[:, at] = (inv * (ngr - normed * mean)).astype(BF)
        out_ref[:, cols + h * HD : cols + (h + 1) * HD] = (
            cot * normed * gain * silu_grad(up)
        ).astype(BF)


def slope_kernel(slots, rows, me_ref, counts_ref, lens_ref, live_ref, query_ref, key_ref, out_ref):
    k = pl.program_id(0)
    width = key_ref.shape[1]
    me = me_ref[0]
    first = (me * pl.num_programs(0) + k) * width
    keep = keep_mask(slots, rows, width, first, me, counts_ref, lens_ref, live_ref[...])
    for h in range(query_ref.shape[1] // HD):
        at = slice(h * HD, (h + 1) * HD)
        half = dot_nt(query_ref[:, at], key_ref[0, :, at]) * (0.5 * SCALE)
        t = jnp.tanh(half)
        slope = 1.0 + t + half * (1.0 - t * t)
        out_ref[h] = jnp.where(keep, slope, 0.0).astype(BF)


def split(v):
    high = v.astype(BF)
    return high, (v - high.astype(F32)).astype(BF)


def backward_kernel(slots, me_ref, *refs):
    grad_refs, pack_refs = refs[:slots], refs[slots : 2 * slots]
    refs = refs[2 * slots :]
    slope_ref, key_ref, value_ref, upt_ref = refs[:4]
    tile_refs = refs[4 : 4 + slots]
    acc_ref, grad_ref = refs[4 + slots :]
    k = pl.program_id(0)
    cands, cols = acc_ref.shape
    rows = cands // slots
    me = me_ref[0]

    @pl.when(k == 0)
    def _():
        acc_ref[...] = jnp.zeros_like(acc_ref)
        for m in range(slots):
            grad_ref[m * rows : (m + 1) * rows, :] = grad_refs[m][:, :cols]

    for h in range(cols // HD):
        at = slice(h * HD, (h + 1) * HD)
        along = dot_nt(grad_ref[:, at], value_ref[0, :, at])
        score_grad = (slope_ref[h].astype(F32) * along).astype(BF)
        acc_ref[:, at] += dot_nn(score_grad, key_ref[0, :, at])

    @pl.when(k == pl.num_programs(0) - 1)
    def _():
        pre_slope = jnp.concatenate([r[:, :cols] for r in pack_refs], axis=0).astype(F32)
        high, low = split(acc_ref[...] * (0.5 * SCALE) * pre_slope)
        up_grad = jnp.concatenate([r[:, cols:] for r in grad_refs], axis=0)
        own = jnp.concatenate([r[:, cols : cols + 1] for r in pack_refs], axis=0).astype(F32)
        row = jnp.concatenate([r[:, cols + 1 : cols + 2] for r in pack_refs], axis=0).astype(F32)
        at_row = lax.broadcasted_iota(jnp.int32, (cands, ITEMS_DEV), 1).astype(F32)
        here = row == at_row
        for m in range(slots):
            mine = own == (me ^ m).astype(F32)
            pick = jnp.where(here & mine, 1.0, 0.0).astype(BF)
            tile_refs[m][...] = (dot_tn(pick, high) + dot_tn(pick, low)).astype(tile_refs[m].dtype)
            if m == 0:
                upt_ref[...] = dot_tn(pick, up_grad)


def weight_kernel(slots, terms, me_ref, upt_ref, *refs):
    term_refs, w_ref = refs[:terms], refs[terms]
    out_refs = refs[terms + 1 : terms + 1 + slots]
    sum_ref, up_ref = refs[terms + 1 + slots :]
    k = pl.program_id(0)
    items = upt_ref.shape[0]

    @pl.when(k == 0)
    def _():
        total = term_refs[0][...]
        for r in term_refs[1:]:
            total = total + r[...].astype(F32)
        sum_ref[:items, :], sum_ref[items:, :] = split(total)
        up_ref[:items, :], up_ref[items:, :] = split(upt_ref[...])

    part = dot_nt(sum_ref[...], w_ref[0]) + dot_nt(up_ref[...], w_ref[1])
    part = part[:items, :] + part[items:, :]
    for m in range(slots):

        @pl.when(k == m)
        def _():
            out_refs[m][...] = part.astype(out_refs[m].dtype)


def body(
    cand_feat,
    cand_counts,
    proj_weight,
    norm_gain,
    hist_kv,
    hist_lens,
    hist_mask,
    out_cot,
    owner,
    item_row,
):
    rows, depth = cand_feat.shape
    slots = lax.axis_size("blk")
    wide = lax.axis_size("heads")
    cols = proj_weight.shape[2]
    heads = cols // HD
    cands = rows * slots
    keys = hist_kv.shape[1]
    me = lax.axis_index("blk").astype(jnp.int32).reshape(1)
    head_me = lax.axis_index("heads").astype(jnp.int32).reshape(1)
    live = hist_mask.reshape(1, keys)
    kstep = min(512, depth)
    width = min(512, keys)
    chunks = keys // width
    sds = jax.ShapeDtypeStruct

    x_spec = pl.BlockSpec((rows, kstep), lambda k: (0, k))
    block = vmem_full((rows, cols))
    every = vmem_full((cands, cols))
    query, pre = pl.pallas_call(
        proj_query_kernel,
        grid=(depth // kstep,),
        in_specs=[x_spec, pl.BlockSpec((1, kstep, cols), lambda k: (0, k, 0))],
        out_specs=[block, block],
        out_shape=[sds((rows, cols), BF), sds((rows, cols), F32)],
        name="proj_query",
    )(cand_feat, proj_weight)
    query_slots = gather_slots(query, "blk")

    up = pl.pallas_call(
        proj_up_kernel,
        grid=(depth // kstep,),
        in_specs=[x_spec, pl.BlockSpec((1, kstep, cols), lambda k: (1, k, 0))],
        out_specs=block,
        out_shape=sds((rows, cols), F32),
        name="proj_up",
    )(cand_feat, proj_weight)
    lane = lax.broadcasted_iota(jnp.int32, (rows, IDX_LANES), 1)
    idx = jnp.where(lane == 0, owner, item_row[:, None]).astype(BF)

    key_spec = pl.BlockSpec((1, width, cols), lambda k: (0, k, 0))
    value_spec = pl.BlockSpec((1, width, cols), lambda k: (1, k, 0))
    live_spec = pl.BlockSpec((1, width), lambda k: (0, k))
    pack_shape = (rows, cols + IDX_LANES)
    outs = pl.pallas_call(
        functools.partial(forward_kernel, slots),
        grid=(chunks,),
        in_specs=[smem_spec()] * 3
        + [live_spec, block, vmem_full((rows, IDX_LANES))]
        + [block] * slots
        + [key_spec, value_spec],
        out_specs=[vmem_full(pack_shape), every] + [block] * slots,
        out_shape=[sds(pack_shape, BF), sds((cands, cols), BF), sds((rows, cols), F32)]
        + [sds((rows, cols), BF)] * (slots - 1),
        scratch_shapes=[pltpu.VMEM((cands, cols), F32)],
        name="attend",
    )(me, cand_counts, hist_lens, live, pre, idx, *query_slots, hist_kv, hist_kv)
    pack, queries = outs[:2]
    terms = scatter_slots(list(outs[2:]), "blk")
    pack_slots = gather_slots(pack, "blk")

    attended, grads = pl.pallas_call(
        functools.partial(norm_kernel, len(terms)),
        out_shape=[sds((rows, cols), BF), sds((rows, 2 * cols), BF)],
        name="norm",
    )(*terms, up, out_cot, norm_gain.reshape(1, cols))
    grad_slots = gather_slots(grads, "blk")

    slope = pl.pallas_call(
        functools.partial(slope_kernel, slots, rows),
        grid=(chunks,),
        in_specs=[smem_spec()] * 3 + [live_spec, every, key_spec],
        out_specs=pl.BlockSpec((heads, cands, width), lambda k: (0, 0, k)),
        out_shape=sds((heads, cands, keys), BF),
        name="slope",
    )(me, cand_counts, hist_lens, live, queries, hist_kv)

    tile = vmem_full((ITEMS_DEV, cols))
    outs = pl.pallas_call(
        functools.partial(backward_kernel, slots),
        grid=(chunks,),
        in_specs=[smem_spec()]
        + [vmem_full((rows, 2 * cols))] * slots
        + [vmem_full(pack_shape)] * slots
        + [pl.BlockSpec((heads, cands, width), lambda k: (0, 0, k)), key_spec, value_spec],
        out_specs=[tile] * (1 + slots),
        out_shape=[sds((ITEMS_DEV, cols), F32)] * 2 + [sds((ITEMS_DEV, cols), BF)] * (slots - 1),
        scratch_shapes=[pltpu.VMEM((cands, cols), F32), pltpu.VMEM((cands, cols), BF)],
        name="attend_grad",
    )(me, *grad_slots, *pack_slots, slope, hist_kv, hist_kv)
    up_table = outs[0]
    terms = scatter_slots(list(outs[1:]), "blk")

    out_cols = depth // wide
    parts = pl.pallas_call(
        functools.partial(weight_kernel, wide, len(terms)),
        grid_spec=pltpu.PrefetchScalarGridSpec(
            num_scalar_prefetch=1,
            grid=(wide,),
            in_specs=[tile] * (1 + len(terms))
            + [pl.BlockSpec((2, out_cols, cols), lambda k, at: (0, at[0] ^ k, 0))],
            out_specs=[vmem_full((ITEMS_DEV, out_cols))] * wide,
            scratch_shapes=[pltpu.VMEM((2 * ITEMS_DEV, cols), BF)] * 2,
        ),
        out_shape=[sds((ITEMS_DEV, out_cols), F32)]
        + [sds((ITEMS_DEV, out_cols), BF)] * (wide - 1),
        name="weight_grad",
    )(head_me, up_table, *terms, proj_weight)
    ends = scatter_slots(list(parts), "heads")
    item_grad = ends[0]
    for e in ends[1:]:
        item_grad = item_grad + e.astype(F32)
    return (attended, item_grad)


def solution(mesh):
    return jax.shard_map(
        body,
        mesh=mesh,
        in_specs=(
            P(("groups", "blk"), None),
            P("groups"),
            P(None, None, "heads"),
            P("heads"),
            P(None, ("groups", "blk"), "heads"),
            P("groups"),
            P(("groups", "blk")),
            P(("groups", "blk"), "heads"),
            P(("groups", "blk"), None),
            P(("groups", "blk")),
        ),
        out_specs=(P(("groups", "blk"), "heads"), P(("groups", "blk"), "heads")),
        check_vma=False,
    )
```

```python
import functools

import jax
import jax.numpy as jnp
from jax import lax
from jax.experimental import pallas as pl
from jax.experimental.pallas import tpu as pltpu
from jax.sharding import PartitionSpec as P


HD = 128
ITEMS_DEV = 48
NORM_EPS = 1e-05
SCALE = HD ** (-0.5)
IDX_LANES = 128
DIRECT = 4
GRANT = 24 << 20

BF = jnp.bfloat16
F32 = jnp.float32
VMEM = pltpu.MemorySpace.VMEM
SMEM = pltpu.MemorySpace.SMEM
HBM = pltpu.MemorySpace.HBM


def silu(v):
    half = v * 0.5
    return half * jnp.tanh(half) + half


def silu_grad(v):
    half = v * 0.5
    t = jnp.tanh(half)
    return 0.5 * (1.0 + t + half * (1.0 - t * t))


def dot_nt(a, b):
    return lax.dot_general(a, b, (((1,), (1,)), ((), ())), preferred_element_type=F32)


def dot_nn(a, b):
    return lax.dot_general(a, b, (((1,), (0,)), ((), ())), preferred_element_type=F32)


def dot_tn(a, b):
    return lax.dot_general(a, b, (((0,), (0,)), ((), ())), preferred_element_type=F32)


def vmem_spec():
    return pl.BlockSpec(memory_space=VMEM)


def smem_spec():
    return pl.BlockSpec(memory_space=SMEM)


def near(x):
    return pltpu.with_memory_space_constraint(x, VMEM)


def far(x):
    return pltpu.with_memory_space_constraint(x, HBM)


LOADS = 4


def load_kernel(src_ref, dst_ref, sems):
    step = src_ref.shape[1] // (LOADS // 2)
    copies = [
        pltpu.make_async_copy(
            src_ref.at[i // 2, pl.ds(i % 2 * step, step)],
            dst_ref.at[i // 2, pl.ds(i % 2 * step, step)],
            sems.at[i],
        )
        for i in range(LOADS)
    ]
    for c in copies:
        c.start()
    for c in copies:
        c.wait()


def load(x):
    return pl.pallas_call(
        load_kernel,
        in_specs=[pl.BlockSpec(memory_space=HBM)],
        out_specs=vmem_spec(),
        out_shape=pltpu.VMEM(x.shape, x.dtype),
        scratch_shapes=[pltpu.SemaphoreType.DMA((LOADS,))],
        compiler_params=pltpu.CompilerParams(vmem_limit_bytes=GRANT),
    )(far(x))


def call(kernel, scalars, arrays, outs, scratch=()):
    return pl.pallas_call(
        kernel,
        in_specs=[smem_spec()] * len(scalars) + [vmem_spec()] * len(arrays),
        out_specs=[vmem_spec()] * len(outs),
        out_shape=[pltpu.VMEM(shape, kind) for shape, kind in outs],
        scratch_shapes=[pltpu.VMEM(shape, kind) for shape, kind in scratch],
        compiler_params=pltpu.CompilerParams(vmem_limit_bytes=GRANT),
    )(*scalars, *[near(x) for x in arrays])


def slot_order(axis):
    return lax.axis_index(axis) ^ jnp.arange(lax.axis_size(axis), dtype=jnp.int32)


def send(x, axis, m):
    return lax.ppermute(x, axis, [(j, j ^ m) for j in range(lax.axis_size(axis))])


def gather_slots(x, axis):
    n = lax.axis_size(axis)
    if n <= DIRECT:
        return [x] + [send(x, axis, m) for m in range(1, n)]
    whole = lax.all_gather(x, axis)[slot_order(axis)]
    return [whole[m] for m in range(n)]


def scatter_slots(tiles, axis):
    n = lax.axis_size(axis)
    if n <= DIRECT:
        return [tiles[0]] + [send(tiles[m], axis, m) for m in range(1, n)]
    stacked = jnp.stack([t.astype(F32) for t in tiles])[slot_order(axis)]
    return [lax.psum_scatter(stacked, axis, scatter_dimension=0, tiled=False)]


def split(v):
    high = v.astype(BF)
    return high, (v - high.astype(F32)).astype(BF)


def project_kernel(owner_ref, row_ref, x_ref, w_ref, cot_ref, query_ref, pack_ref, up_ref, pre_ref):
    k = pl.program_id(0)
    rows, cols = up_ref.shape

    @pl.when(k == 0)
    def _():
        pre_ref[...] = jnp.zeros_like(pre_ref)
        up_ref[...] = jnp.zeros_like(up_ref)
        lane = lax.broadcasted_iota(jnp.int32, (rows, IDX_LANES), 1)
        line = lax.broadcasted_iota(jnp.int32, (rows, IDX_LANES), 0)
        idx = jnp.zeros((rows, IDX_LANES), jnp.int32)
        for r in range(rows):
            idx = jnp.where(line == r, jnp.where(lane == 0, owner_ref[r], row_ref[r]), idx)
        pack_ref[:, 3 * cols :] = idx.astype(F32).astype(BF)
        pack_ref[:, :cols] = cot_ref[...]

    pre_ref[...] += dot_nn(x_ref[...], w_ref[0])
    up_ref[...] += dot_nn(x_ref[...], w_ref[1])

    @pl.when(k == pl.num_programs(0) - 1)
    def _():
        query_ref[...] = silu(pre_ref[...]).astype(BF)
        pack_ref[:, cols : 2 * cols] = up_ref[...].astype(BF)
        pack_ref[:, 2 * cols : 3 * cols] = silu_grad(pre_ref[...]).astype(BF)


def user_of(pos, counts_ref):
    user = jnp.zeros_like(pos)
    end = jnp.int32(0)
    for u in range(counts_ref.shape[0]):
        end = end + counts_ref[u]
        user = user + (pos >= end).astype(jnp.int32)
    return user


def keep_mask(slots, rows, width, first_key, me, counts_ref, lens_ref, live):
    cand = jnp.concatenate(
        [
            lax.broadcasted_iota(jnp.int32, (rows, 1), 0) + (me ^ m) * rows
            for m in range(slots)
        ],
        axis=0,
    )
    key = lax.broadcasted_iota(jnp.int32, (1, width), 1) + first_key
    key_user = jnp.where(live > 0, user_of(key, lens_ref), -1)
    return user_of(cand, counts_ref) == key_user


def diagonal(ref, first, heads):
    parts = [ref[:, (first + h) * HD : (first + h + 1) * HD] for h in range(heads)]
    none = jnp.zeros_like(parts[0])
    return jnp.concatenate(
        [
            jnp.concatenate([parts[h] if h == g else none for g in range(heads)], axis=1)
            for h in range(heads)
        ],
        axis=0,
    )


def chunk_mask(slots, rows, k, width, together, me, counts_ref, lens_ref, live_ref, keys):
    live = live_ref[:, k * width : (k + 1) * width]
    first = me * keys + k * width
    keep = keep_mask(slots, rows, width, first, me, counts_ref, lens_ref, live)
    return jnp.concatenate([keep] * together, axis=0)


def forward_kernel(
    slots, together, width, me_ref, counts_ref, lens_ref, live_ref, kv_ref, *refs
):
    got_refs = refs[:slots]
    sum_ref, low_ref, query_ref = refs[slots:]
    cands, cols = sum_ref.shape
    rows = cands // slots
    keys = kv_ref.shape[1]
    me = me_ref[0]
    for m in range(slots):
        query_ref[m * rows : (m + 1) * rows, :] = got_refs[m][...]
    for p in range(0, cols // HD, together):
        at = slice(p * HD, (p + together) * HD)
        query = diagonal(query_ref, p, together)
        total = jnp.zeros((together * cands, together * HD), F32)
        for k in range(keys // width):
            ks = slice(k * width, (k + 1) * width)
            keep = chunk_mask(
                slots, rows, k, width, together, me, counts_ref, lens_ref, live_ref, keys
            )
            half = dot_nt(query, kv_ref[0, ks, at]) * (0.5 * SCALE)
            att = jnp.where(keep, half * jnp.tanh(half) + half, 0.0).astype(BF)
            total = total + dot_nn(att, kv_ref[1, ks, at])
        for h in range(together):
            part = total[h * cands : (h + 1) * cands, h * HD : (h + 1) * HD]
            hs = slice((p + h) * HD, (p + h + 1) * HD)
            sum_ref[:, hs] = part
            low_ref[:, hs] = part.astype(BF)


def slope_kernel(
    slots, together, width, me_ref, counts_ref, lens_ref, live_ref, kv_ref, query_ref, out_ref
):
    cands, cols = query_ref.shape
    keys = kv_ref.shape[1]
    me = me_ref[0]
    for p in range(0, cols // HD, together):
        at = slice(p * HD, (p + together) * HD)
        query = diagonal(query_ref, p, together)
        for k in range(keys // width):
            ks = slice(k * width, (k + 1) * width)
            keep = chunk_mask(
                slots, cands // slots, k, width, together, me, counts_ref, lens_ref, live_ref, keys
            )
            half = dot_nt(query, kv_ref[0, ks, at]) * (0.5 * SCALE)
            t = jnp.tanh(half)
            slope = 1.0 + t + half * (1.0 - t * t)
            out_ref[p * cands : (p + together) * cands, ks] = jnp.where(keep, slope, 0.0).astype(BF)


def backward_kernel(slots, together, width, me_ref, gain_ref, up_ref, sum_ref, kv_ref, slope_ref, *refs):
    got, pack_refs = refs[: len(refs) - 2 * slots - 5], refs[len(refs) - 2 * slots - 5 :][:slots]
    refs = refs[len(refs) - slots - 5 :]
    att_ref, upt_ref = refs[:2]
    tile_refs = refs[2 : 2 + slots]
    acc_ref, grad_ref, ug_ref = refs[2 + slots :]
    rows, cols = up_ref.shape
    cands = rows * slots
    keys = kv_ref.shape[1]
    me = me_ref[0]

    for s in range(slots):
        block = slice(s * rows, (s + 1) * rows)
        total = sum_ref[block, :]
        for m in range(1, len(got) + 1):
            other = s ^ m
            total = total + got[m - 1][other * rows : (other + 1) * rows, :].astype(F32)
        for h in range(cols // HD):
            at = slice(h * HD, (h + 1) * HD)
            part = total[:, at]
            inv = lax.rsqrt(jnp.mean(part * part, axis=-1, keepdims=True) + NORM_EPS)
            normed = part * inv
            gain = gain_ref[:, at].astype(F32)
            cot = pack_refs[s][:, at].astype(F32)
            if s == 0:
                up = up_ref[:, at]
            else:
                up = pack_refs[s][:, cols + h * HD : cols + (h + 1) * HD].astype(F32)
            gate = silu(up)
            if s == 0:
                att_ref[:, at] = (normed * gain * gate).astype(BF)
            ug_ref[block, at] = (cot * normed * gain * silu_grad(up)).astype(BF)
            ngr = cot * gate * gain
            mean = jnp.mean(ngr * normed, axis=-1, keepdims=True)
            grad_ref[block, at] = (inv * (ngr - normed * mean)).astype(BF)

    for p in range(0, cols // HD, together):
        at = slice(p * HD, (p + together) * HD)
        grad = diagonal(grad_ref, p, together)
        total = jnp.zeros((together * cands, together * HD), F32)
        for k in range(keys // width):
            ks = slice(k * width, (k + 1) * width)
            along = dot_nt(grad, kv_ref[1, ks, at])
            slope = slope_ref[p * cands : (p + together) * cands, ks].astype(F32)
            total = total + dot_nn((slope * along).astype(BF), kv_ref[0, ks, at])
        for h in range(together):
            hs = slice((p + h) * HD, (p + h + 1) * HD)
            acc_ref[:, hs] = total[h * cands : (h + 1) * cands, h * HD : (h + 1) * HD]

    pre_slope = jnp.concatenate([r[:, 2 * cols : 3 * cols] for r in pack_refs], axis=0).astype(F32)
    high, low = split(acc_ref[...] * (0.5 * SCALE) * pre_slope)
    idx = jnp.concatenate([r[:, 3 * cols :] for r in pack_refs], axis=0).astype(F32)
    own, row = idx[:, :1], idx[:, 1:2]
    at_row = lax.broadcasted_iota(jnp.int32, (cands, ITEMS_DEV), 1).astype(F32)
    here = row == at_row
    for m in range(slots):
        mine = own == (me ^ m).astype(F32)
        pick = jnp.where(here & mine, 1.0, 0.0).astype(BF)
        tile_refs[m][...] = (dot_tn(pick, high) + dot_tn(pick, low)).astype(tile_refs[m].dtype)
        if m == 0:
            upt_ref[...] = dot_tn(pick, ug_ref[...])


def weight_kernel(slots, terms, me_ref, w_ref, upt_ref, *refs):
    term_refs, out_refs = refs[:terms], refs[terms:]
    items = upt_ref.shape[0]
    height = out_refs[0].shape[1]
    total = term_refs[0][...]
    for r in term_refs[1:]:
        total = total + r[...].astype(F32)
    table = jnp.concatenate(split(total), axis=0)
    ups = jnp.concatenate(split(upt_ref[...]), axis=0)
    for m in range(slots):
        at = pl.ds(pl.multiple_of((me_ref[0] ^ m) * height, height), height)
        part = dot_nt(table, w_ref[0, at, :]) + dot_nt(ups, w_ref[1, at, :])
        out_refs[m][...] = (part[:items, :] + part[items:, :]).astype(out_refs[m].dtype)


def finish_kernel(*refs):
    total = refs[0][...]
    for r in refs[1:-1]:
        total = total + r[...].astype(F32)
    refs[-1][...] = total


def whole_body(
    cand_feat,
    cand_counts,
    proj_weight,
    norm_gain,
    hist_kv,
    hist_lens,
    hist_mask,
    out_cot,
    owner,
    item_row,
):
    rows, depth = cand_feat.shape
    slots = lax.axis_size("blk")
    wide = lax.axis_size("heads")
    cols = proj_weight.shape[2]
    heads = cols // HD
    cands = rows * slots
    keys = hist_kv.shape[1]
    me = lax.axis_index("blk").astype(jnp.int32).reshape(1)
    head_me = lax.axis_index("heads").astype(jnp.int32).reshape(1)
    live = hist_mask.reshape(1, keys)
    kstep = min(512, depth)
    width = min(512, keys)

    together = 2 if heads % 2 == 0 else 1
    pack_cols = 3 * cols + IDX_LANES
    query, pack, up = pl.pallas_call(
        project_kernel,
        grid=(depth // kstep,),
        in_specs=[
            smem_spec(),
            smem_spec(),
            pl.BlockSpec((rows, kstep), lambda k: (0, k)),
            pl.BlockSpec((2, kstep, cols), lambda k: (0, k, 0)),
            pl.BlockSpec((rows, cols), lambda k: (0, 0)),
        ],
        out_specs=[vmem_spec()] * 3,
        out_shape=[
            pltpu.VMEM((rows, cols), BF),
            pltpu.VMEM((rows, pack_cols), BF),
            pltpu.VMEM((rows, cols), F32),
        ],
        scratch_shapes=[pltpu.VMEM((rows, cols), F32)],
        compiler_params=pltpu.CompilerParams(vmem_limit_bytes=GRANT),
        name="project",
    )(owner.reshape(rows), item_row, far(cand_feat), far(proj_weight), far(out_cot))
    query_slots = gather_slots(query, "blk")
    pack_slots = gather_slots(pack, "blk")

    hist_kv = load(hist_kv)
    weight = load(proj_weight)

    every = (cands, cols)
    ranges = [me, cand_counts, hist_lens]
    sums, low, queries = call(
        functools.partial(forward_kernel, slots, together, width),
        ranges,
        [live, hist_kv, *query_slots],
        [(every, F32), (every, BF), (every, BF)],
    )
    if slots <= DIRECT:
        got = [send(low, "blk", m) for m in range(1, slots)]
    else:
        order = slot_order("blk")
        whole = lax.psum(sums.reshape(slots, rows, cols)[order], "blk")
        sums, got = whole[order].reshape(cands, cols), []

    slope = call(
        functools.partial(slope_kernel, slots, together, width),
        ranges,
        [live, hist_kv, queries],
        [((heads * cands, keys), BF)],
    )[0]

    tile = (ITEMS_DEV, cols)
    outs = call(
        functools.partial(backward_kernel, slots, together, width),
        [me],
        [norm_gain.reshape(1, cols), up, sums, hist_kv, slope, *got, *pack_slots],
        [((rows, cols), BF), (tile, F32), (tile, F32)] + [(tile, BF)] * (slots - 1),
        [(every, F32), (every, BF), (every, BF)],
    )
    attended, up_table = outs[:2]
    terms = scatter_slots(list(outs[2:]), "blk")

    end = (ITEMS_DEV, depth // wide)
    parts = call(
        functools.partial(weight_kernel, wide, len(terms)),
        [head_me],
        [weight, up_table, *terms],
        [(end, F32)] + [(end, BF)] * (wide - 1),
    )
    ends = scatter_slots(list(parts), "heads")
    item_grad = call(finish_kernel, [], ends, [(end, F32)])[0]
    return (attended, item_grad)


def solution(mesh):
    return jax.shard_map(
        whole_body,
        mesh=mesh,
        in_specs=(
            P(("groups", "blk"), None),
            P("groups"),
            P(None, None, "heads"),
            P("heads"),
            P(None, ("groups", "blk"), "heads"),
            P("groups"),
            P(("groups", "blk")),
            P(("groups", "blk"), "heads"),
            P(("groups", "blk"), None),
            P(("groups", "blk")),
        ),
        out_specs=(P(("groups", "blk"), "heads"), P(("groups", "blk"), "heads")),
        check_vma=False,
    )
```

```python
import functools

import jax
import jax.numpy as jnp
from jax import lax
from jax.experimental import pallas as pl
from jax.experimental.pallas import tpu as pltpu
from jax.sharding import PartitionSpec as P


HD = 128
ITEMS_DEV = 48
NORM_EPS = 1e-05
SCALE = HD ** (-0.5)
IDX_LANES = 128
DIRECT = 4
GRANT = 24 << 20

BF = jnp.bfloat16
F32 = jnp.float32
VMEM = pltpu.MemorySpace.VMEM
SMEM = pltpu.MemorySpace.SMEM
HBM = pltpu.MemorySpace.HBM


def silu(v):
    half = v * 0.5
    return half * jnp.tanh(half) + half


def silu_grad(v):
    half = v * 0.5
    t = jnp.tanh(half)
    return 0.5 * (1.0 + t + half * (1.0 - t * t))


def dot_nt(a, b):
    return lax.dot_general(a, b, (((1,), (1,)), ((), ())), preferred_element_type=F32)


def dot_nn(a, b):
    return lax.dot_general(a, b, (((1,), (0,)), ((), ())), preferred_element_type=F32)


def dot_tn(a, b):
    return lax.dot_general(a, b, (((0,), (0,)), ((), ())), preferred_element_type=F32)


def vmem_spec():
    return pl.BlockSpec(memory_space=VMEM)


def smem_spec():
    return pl.BlockSpec(memory_space=SMEM)


def near(x):
    return pltpu.with_memory_space_constraint(x, VMEM)


def far(x):
    return pltpu.with_memory_space_constraint(x, HBM)


LOADS = 4
PARTS = 4


def load_kernel(src_ref, dst_ref, sems):
    step = src_ref.shape[1] // (LOADS // 2)
    copies = [
        pltpu.make_async_copy(
            src_ref.at[i // 2, pl.ds(i % 2 * step, step)],
            dst_ref.at[i // 2, pl.ds(i % 2 * step, step)],
            sems.at[i],
        )
        for i in range(LOADS)
    ]
    for c in copies:
        c.start()
    for c in copies:
        c.wait()


def load(x):
    return pl.pallas_call(
        load_kernel,
        in_specs=[pl.BlockSpec(memory_space=HBM)],
        out_specs=vmem_spec(),
        out_shape=pltpu.VMEM(x.shape, x.dtype),
        scratch_shapes=[pltpu.SemaphoreType.DMA((LOADS,))],
        compiler_params=pltpu.CompilerParams(vmem_limit_bytes=GRANT),
    )(far(x))


def call(kernel, scalars, arrays, outs, scratch=()):
    return pl.pallas_call(
        kernel,
        in_specs=[smem_spec()] * len(scalars) + [vmem_spec()] * len(arrays),
        out_specs=[vmem_spec()] * len(outs),
        out_shape=[pltpu.VMEM(shape, kind) for shape, kind in outs],
        scratch_shapes=[pltpu.VMEM(shape, kind) for shape, kind in scratch],
        compiler_params=pltpu.CompilerParams(vmem_limit_bytes=GRANT),
    )(*scalars, *[near(x) for x in arrays])


def slot_order(axis):
    return lax.axis_index(axis) ^ jnp.arange(lax.axis_size(axis), dtype=jnp.int32)


def send(x, axis, m):
    return lax.ppermute(x, axis, [(j, j ^ m) for j in range(lax.axis_size(axis))])


def gather_slots(x, axis):
    n = lax.axis_size(axis)
    if n <= DIRECT:
        return [x] + [send(x, axis, m) for m in range(1, n)]
    whole = lax.all_gather(x, axis)[slot_order(axis)]
    return [whole[m] for m in range(n)]


def scatter_slots(tiles, axis):
    n = lax.axis_size(axis)
    if n <= DIRECT:
        return [tiles[0]] + [send(tiles[m], axis, m) for m in range(1, n)]
    stacked = jnp.stack([t.astype(F32) for t in tiles])[slot_order(axis)]
    return [lax.psum_scatter(stacked, axis, scatter_dimension=0, tiled=False)]


def split(v):
    high = v.astype(BF)
    return high, (v - high.astype(F32)).astype(BF)


def column(line_ref):
    n = line_ref.shape[1]
    same = lax.broadcasted_iota(jnp.int32, (n, n), 0) == lax.broadcasted_iota(jnp.int32, (n, n), 1)
    return jnp.sum(jnp.where(same, line_ref[...], 0).astype(F32), axis=1, keepdims=True)


def project_kernel(
    x_hbm, w_hbm, cot_hbm, owner_hbm, row_hbm, query_ref, pack_ref, both_ref, up_ref,
    x_ref, w_ref, owner_ref, row_ref, sems,
):
    rows, cols = up_ref.shape
    depth = x_ref.shape[1]
    step = depth // PARTS
    copies = []

    def start(src, dst):
        copies.append(pltpu.make_async_copy(src, dst, sems.at[len(copies)]))
        copies[-1].start()

    start(x_hbm, x_ref)
    for j in range(2):
        for i in range(PARTS):
            at = pl.ds(i * step, step)
            start(w_hbm.at[j, at], w_ref.at[j, at])
    start(cot_hbm, pack_ref.at[:, pl.ds(0, cols)])
    start(owner_hbm, owner_ref)
    start(row_hbm, row_ref)
    copies[0].wait()

    def product(j):
        total = jnp.zeros((rows, cols), F32)
        for i in range(PARTS):
            copies[1 + j * PARTS + i].wait()
            at = slice(i * step, (i + 1) * step)
            total = total + dot_nn(x_ref[:, at], w_ref[j, at, :])
        return total

    pre = product(0)
    query_ref[...] = silu(pre).astype(BF)
    pack_ref[:, 2 * cols : 3 * cols] = silu_grad(pre).astype(BF)
    up = product(1)
    up_ref[...] = up
    pack_ref[:, cols : 2 * cols] = up.astype(BF)
    for c in copies[1 + 2 * PARTS :]:
        c.wait()
    lane = lax.broadcasted_iota(jnp.int32, (rows, IDX_LANES), 1)
    idx = jnp.where(lane == 0, column(owner_ref), column(row_ref))
    pack_ref[:, 3 * cols :] = idx.astype(BF)
    both_ref[:, :cols] = query_ref[...]
    both_ref[:, cols:] = pack_ref[...]


def user_of(pos, counts_ref):
    user = jnp.zeros_like(pos)
    end = jnp.int32(0)
    for u in range(counts_ref.shape[0]):
        end = end + counts_ref[u]
        user = user + (pos >= end).astype(jnp.int32)
    return user


def keep_mask(slots, rows, width, first_key, me, counts_ref, lens_ref, live):
    cand = jnp.concatenate(
        [
            lax.broadcasted_iota(jnp.int32, (rows, 1), 0) + (me ^ m) * rows
            for m in range(slots)
        ],
        axis=0,
    )
    key = lax.broadcasted_iota(jnp.int32, (1, width), 1) + first_key
    key_user = jnp.where(live > 0, user_of(key, lens_ref), -1)
    return user_of(cand, counts_ref) == key_user


def diagonal(ref, first, heads):
    parts = [ref[:, (first + h) * HD : (first + h + 1) * HD] for h in range(heads)]
    none = jnp.zeros_like(parts[0])
    return jnp.concatenate(
        [
            jnp.concatenate([parts[h] if h == g else none for g in range(heads)], axis=1)
            for h in range(heads)
        ],
        axis=0,
    )


def chunk_mask(slots, rows, k, width, together, me, counts_ref, lens_ref, live_ref, keys):
    live = live_ref[:, k * width : (k + 1) * width]
    first = me * keys + k * width
    keep = keep_mask(slots, rows, width, first, me, counts_ref, lens_ref, live)
    return jnp.concatenate([keep] * together, axis=0)


def forward_kernel(
    slots, together, width, me_ref, counts_ref, lens_ref, live_ref, kv_ref, *refs
):
    got_refs = refs[:slots]
    sum_ref, low_ref, query_ref = refs[slots:]
    cands, cols = sum_ref.shape
    rows = cands // slots
    keys = kv_ref.shape[1]
    me = me_ref[0]
    for m in range(slots):
        query_ref[m * rows : (m + 1) * rows, :] = got_refs[m][:, :cols]
    for p in range(0, cols // HD, together):
        at = slice(p * HD, (p + together) * HD)
        query = diagonal(query_ref, p, together)
        total = jnp.zeros((together * cands, together * HD), F32)
        for k in range(keys // width):
            ks = slice(k * width, (k + 1) * width)
            keep = chunk_mask(
                slots, rows, k, width, together, me, counts_ref, lens_ref, live_ref, keys
            )
            half = dot_nt(query, kv_ref[0, ks, at]) * (0.5 * SCALE)
            att = jnp.where(keep, half * jnp.tanh(half) + half, 0.0).astype(BF)
            total = total + dot_nn(att, kv_ref[1, ks, at])
        for h in range(together):
            part = total[h * cands : (h + 1) * cands, h * HD : (h + 1) * HD]
            hs = slice((p + h) * HD, (p + h + 1) * HD)
            sum_ref[:, hs] = part
            low_ref[:, hs] = part.astype(BF)


def slope_kernel(
    slots, together, width, me_ref, counts_ref, lens_ref, live_ref, kv_ref, query_ref, out_ref
):
    cands, cols = query_ref.shape
    keys = kv_ref.shape[1]
    me = me_ref[0]
    for p in range(0, cols // HD, together):
        at = slice(p * HD, (p + together) * HD)
        query = diagonal(query_ref, p, together)
        for k in range(keys // width):
            ks = slice(k * width, (k + 1) * width)
            keep = chunk_mask(
                slots, cands // slots, k, width, together, me, counts_ref, lens_ref, live_ref, keys
            )
            half = dot_nt(query, kv_ref[0, ks, at]) * (0.5 * SCALE)
            t = jnp.tanh(half)
            slope = 1.0 + t + half * (1.0 - t * t)
            out_ref[p * cands : (p + together) * cands, ks] = jnp.where(keep, slope, 0.0).astype(BF)


def backward_kernel(slots, together, width, me_ref, gain_ref, up_ref, sum_ref, kv_ref, slope_ref, *refs):
    got, pack_refs = refs[: len(refs) - 2 * slots - 5], refs[len(refs) - 2 * slots - 5 :][:slots]
    refs = refs[len(refs) - slots - 5 :]
    att_ref, upt_ref = refs[:2]
    tile_refs = refs[2 : 2 + slots]
    acc_ref, grad_ref, ug_ref = refs[2 + slots :]
    rows, cols = up_ref.shape
    cands = rows * slots
    keys = kv_ref.shape[1]
    me = me_ref[0]
    packs = [r.at[:, pl.ds(r.shape[1] - 3 * cols - IDX_LANES, 3 * cols + IDX_LANES)] for r in pack_refs]

    for s in range(slots):
        block = slice(s * rows, (s + 1) * rows)
        total = sum_ref[block, :]
        for m in range(1, len(got) + 1):
            other = s ^ m
            total = total + got[m - 1][other * rows : (other + 1) * rows, :].astype(F32)
        for h in range(cols // HD):
            at = slice(h * HD, (h + 1) * HD)
            part = total[:, at]
            inv = lax.rsqrt(jnp.mean(part * part, axis=-1, keepdims=True) + NORM_EPS)
            normed = part * inv
            gain = gain_ref[:, at].astype(F32)
            cot = packs[s][:, at].astype(F32)
            if s == 0:
                up = up_ref[:, at]
            else:
                up = packs[s][:, cols + h * HD : cols + (h + 1) * HD].astype(F32)
            gate = silu(up)
            if s == 0:
                att_ref[:, at] = (normed * gain * gate).astype(BF)
            ug_ref[block, at] = (cot * normed * gain * silu_grad(up)).astype(BF)
            ngr = cot * gate * gain
            mean = jnp.mean(ngr * normed, axis=-1, keepdims=True)
            grad_ref[block, at] = (inv * (ngr - normed * mean)).astype(BF)

    for p in range(0, cols // HD, together):
        at = slice(p * HD, (p + together) * HD)
        grad = diagonal(grad_ref, p, together)
        total = jnp.zeros((together * cands, together * HD), F32)
        for k in range(keys // width):
            ks = slice(k * width, (k + 1) * width)
            along = dot_nt(grad, kv_ref[1, ks, at])
            slope = slope_ref[p * cands : (p + together) * cands, ks].astype(F32)
            total = total + dot_nn((slope * along).astype(BF), kv_ref[0, ks, at])
        for h in range(together):
            hs = slice((p + h) * HD, (p + h + 1) * HD)
            acc_ref[:, hs] = total[h * cands : (h + 1) * cands, h * HD : (h + 1) * HD]

    pre_slope = jnp.concatenate([r[:, 2 * cols : 3 * cols] for r in packs], axis=0).astype(F32)
    high, low = split(acc_ref[...] * (0.5 * SCALE) * pre_slope)
    idx = jnp.concatenate([r[:, 3 * cols :] for r in packs], axis=0).astype(F32)
    own, row = idx[:, :1], idx[:, 1:2]
    at_row = lax.broadcasted_iota(jnp.int32, (cands, ITEMS_DEV), 1).astype(F32)
    here = row == at_row
    for m in range(slots):
        mine = own == (me ^ m).astype(F32)
        pick = jnp.where(here & mine, 1.0, 0.0).astype(BF)
        tile_refs[m][...] = (dot_tn(pick, high) + dot_tn(pick, low)).astype(tile_refs[m].dtype)
        if m == 0:
            upt_ref[...] = dot_tn(pick, ug_ref[...])


def weight_kernel(slots, terms, me_ref, w_ref, upt_ref, *refs):
    term_refs, out_refs = refs[:terms], refs[terms:]
    items = upt_ref.shape[0]
    height = out_refs[0].shape[1]
    total = term_refs[0][...]
    for r in term_refs[1:]:
        total = total + r[...].astype(F32)
    table = jnp.concatenate(split(total), axis=0)
    ups = jnp.concatenate(split(upt_ref[...]), axis=0)
    for m in range(slots):
        at = pl.ds(pl.multiple_of((me_ref[0] ^ m) * height, height), height)
        part = dot_nt(table, w_ref[0, at, :]) + dot_nt(ups, w_ref[1, at, :])
        out_refs[m][...] = (part[:items, :] + part[items:, :]).astype(out_refs[m].dtype)


def whole_body(
    cand_feat,
    cand_counts,
    proj_weight,
    norm_gain,
    hist_kv,
    hist_lens,
    hist_mask,
    out_cot,
    owner,
    item_row,
):
    rows, depth = cand_feat.shape
    slots = lax.axis_size("blk")
    wide = lax.axis_size("heads")
    cols = proj_weight.shape[2]
    heads = cols // HD
    cands = rows * slots
    keys = hist_kv.shape[1]
    me = lax.axis_index("blk").astype(jnp.int32).reshape(1)
    head_me = lax.axis_index("heads").astype(jnp.int32).reshape(1)
    live = hist_mask.reshape(1, keys)
    width = min(512, keys)

    together = 2 if heads % 2 == 0 else 1
    pack_cols = 3 * cols + IDX_LANES
    query, pack, both, up = pl.pallas_call(
        project_kernel,
        in_specs=[pl.BlockSpec(memory_space=HBM)] * 5,
        out_specs=[vmem_spec()] * 4,
        out_shape=[
            pltpu.VMEM((rows, cols), BF),
            pltpu.VMEM((rows, pack_cols), BF),
            pltpu.VMEM((rows, cols + pack_cols), BF),
            pltpu.VMEM((rows, cols), F32),
        ],
        scratch_shapes=[
            pltpu.VMEM((rows, depth), BF),
            pltpu.VMEM((2, depth, cols), BF),
            pltpu.VMEM((1, rows), jnp.int32),
            pltpu.VMEM((1, rows), jnp.int32),
            pltpu.SemaphoreType.DMA((2 * PARTS + 4,)),
        ],
        compiler_params=pltpu.CompilerParams(vmem_limit_bytes=GRANT),
        name="project",
    )(
        far(cand_feat),
        far(proj_weight),
        far(out_cot),
        far(owner.reshape(1, rows)),
        far(item_row.reshape(1, rows)),
    )
    if slots == 4:
        near_one = send(both, "blk", 1)
        query_slots = [query, near_one] + [send(query, "blk", m) for m in (2, 3)]
        second = send(pack, "blk", 2)
        pack_slots = [pack, near_one, second, send(second, "blk", 1)]
    else:
        query_slots = gather_slots(query, "blk")
        pack_slots = gather_slots(pack, "blk")

    hist_kv = load(hist_kv)
    weight = load(proj_weight)

    every = (cands, cols)
    ranges = [me, cand_counts, hist_lens]
    sums, low, queries = call(
        functools.partial(forward_kernel, slots, together, width),
        ranges,
        [live, hist_kv, *query_slots],
        [(every, F32), (every, BF), (every, BF)],
    )
    if slots <= DIRECT:
        got = [send(low, "blk", m) for m in range(1, slots)]
    else:
        order = slot_order("blk")
        whole = lax.psum(sums.reshape(slots, rows, cols)[order], "blk")
        sums, got = whole[order].reshape(cands, cols), []

    slope = call(
        functools.partial(slope_kernel, slots, together, width),
        ranges,
        [live, hist_kv, queries],
        [((heads * cands, keys), BF)],
    )[0]

    tile = (ITEMS_DEV, cols)
    outs = call(
        functools.partial(backward_kernel, slots, together, width),
        [me],
        [norm_gain.reshape(1, cols), up, sums, hist_kv, slope, *got, *pack_slots],
        [((rows, cols), BF), (tile, F32), (tile, F32)] + [(tile, BF)] * (slots - 1),
        [(every, F32), (every, BF), (every, BF)],
    )
    attended, up_table = outs[:2]
    terms = scatter_slots(list(outs[2:]), "blk")

    end = (ITEMS_DEV, depth // wide)
    parts = call(
        functools.partial(weight_kernel, wide, len(terms)),
        [head_me],
        [weight, up_table, *terms],
        [(end, F32)] + [(end, BF)] * (wide - 1),
    )
    ends = scatter_slots(list(parts), "heads")
    item_grad = ends[0]
    for e in ends[1:]:
        item_grad = item_grad + e.astype(F32)
    return (attended, item_grad)


def solution(mesh):
    return jax.shard_map(
        whole_body,
        mesh=mesh,
        in_specs=(
            P(("groups", "blk"), None),
            P("groups"),
            P(None, None, "heads"),
            P("heads"),
            P(None, ("groups", "blk"), "heads"),
            P("groups"),
            P(("groups", "blk")),
            P(("groups", "blk"), "heads"),
            P(("groups", "blk"), None),
            P(("groups", "blk")),
        ),
        out_specs=(P(("groups", "blk"), "heads"), P(("groups", "blk"), "heads")),
        check_vma=False,
    )
```

```python
import functools

import jax
import jax.numpy as jnp
from jax import lax
from jax.experimental import pallas as pl
from jax.experimental.pallas import tpu as pltpu
from jax.sharding import PartitionSpec as P


HD = 128
ITEMS_DEV = 48
NORM_EPS = 1e-05
SCALE = HD ** (-0.5)
IDX_LANES = 128
DIRECT = 4
GRANT = 24 << 20

BF = jnp.bfloat16
F32 = jnp.float32
VMEM = pltpu.MemorySpace.VMEM
SMEM = pltpu.MemorySpace.SMEM
HBM = pltpu.MemorySpace.HBM


def silu(v):
    half = v * 0.5
    return half * jnp.tanh(half) + half


def silu_grad(v):
    half = v * 0.5
    t = jnp.tanh(half)
    return 0.5 * (1.0 + t + half * (1.0 - t * t))


def dot_nt(a, b):
    return lax.dot_general(a, b, (((1,), (1,)), ((), ())), preferred_element_type=F32)


def dot_nn(a, b):
    return lax.dot_general(a, b, (((1,), (0,)), ((), ())), preferred_element_type=F32)


def dot_tn(a, b):
    return lax.dot_general(a, b, (((0,), (0,)), ((), ())), preferred_element_type=F32)


def vmem_spec():
    return pl.BlockSpec(memory_space=VMEM)


def smem_spec():
    return pl.BlockSpec(memory_space=SMEM)


def near(x):
    return pltpu.with_memory_space_constraint(x, VMEM)


def far(x):
    return pltpu.with_memory_space_constraint(x, HBM)


LOADS = 4
PARTS = 4


def load_kernel(src_ref, dst_ref, sems):
    step = src_ref.shape[1] // (LOADS // 2)
    copies = [
        pltpu.make_async_copy(
            src_ref.at[i // 2, pl.ds(i % 2 * step, step)],
            dst_ref.at[i // 2, pl.ds(i % 2 * step, step)],
            sems.at[i],
        )
        for i in range(LOADS)
    ]
    for c in copies:
        c.start()
    for c in copies:
        c.wait()


def load(x):
    return pl.pallas_call(
        load_kernel,
        in_specs=[pl.BlockSpec(memory_space=HBM)],
        out_specs=vmem_spec(),
        out_shape=pltpu.VMEM(x.shape, x.dtype),
        scratch_shapes=[pltpu.SemaphoreType.DMA((LOADS,))],
        compiler_params=pltpu.CompilerParams(vmem_limit_bytes=GRANT),
    )(far(x))


def call(kernel, scalars, arrays, outs, scratch=()):
    return pl.pallas_call(
        kernel,
        in_specs=[smem_spec()] * len(scalars) + [vmem_spec()] * len(arrays),
        out_specs=[vmem_spec()] * len(outs),
        out_shape=[pltpu.VMEM(shape, kind) for shape, kind in outs],
        scratch_shapes=[pltpu.VMEM(shape, kind) for shape, kind in scratch],
        compiler_params=pltpu.CompilerParams(vmem_limit_bytes=GRANT),
    )(*scalars, *[near(x) for x in arrays])


def slot_order(axis):
    return lax.axis_index(axis) ^ jnp.arange(lax.axis_size(axis), dtype=jnp.int32)


def send(x, axis, m):
    return lax.ppermute(x, axis, [(j, j ^ m) for j in range(lax.axis_size(axis))])


def gather_slots(x, axis):
    n = lax.axis_size(axis)
    if n <= DIRECT:
        return [x] + [send(x, axis, m) for m in range(1, n)]
    whole = lax.all_gather(x, axis)[slot_order(axis)]
    return [whole[m] for m in range(n)]


def scatter_slots(tiles, axis):
    n = lax.axis_size(axis)
    if n <= DIRECT:
        return [tiles[0]] + [send(tiles[m], axis, m) for m in range(1, n)]
    stacked = jnp.stack([t.astype(F32) for t in tiles])[slot_order(axis)]
    return [lax.psum_scatter(stacked, axis, scatter_dimension=0, tiled=False)]


def split(v):
    high = v.astype(BF)
    return high, (v - high.astype(F32)).astype(BF)


def column(line_ref):
    n = line_ref.shape[1]
    same = lax.broadcasted_iota(jnp.int32, (n, n), 0) == lax.broadcasted_iota(jnp.int32, (n, n), 1)
    return jnp.sum(jnp.where(same, line_ref[...], 0).astype(F32), axis=1, keepdims=True)


def project_kernel(
    x_hbm, w_hbm, cot_hbm, owner_hbm, row_hbm, query_ref, pack_ref, up_ref,
    x_ref, w_ref, owner_ref, row_ref, sems,
):
    rows, cols = up_ref.shape
    depth = x_ref.shape[1]
    step = depth // PARTS
    copies = []

    def start(src, dst):
        copies.append(pltpu.make_async_copy(src, dst, sems.at[len(copies)]))
        copies[-1].start()

    start(x_hbm, x_ref)
    for j in range(2):
        for i in range(PARTS):
            at = pl.ds(i * step, step)
            start(w_hbm.at[j, at], w_ref.at[j, at])
    start(cot_hbm, pack_ref.at[:, pl.ds(0, cols)])
    start(owner_hbm, owner_ref)
    start(row_hbm, row_ref)
    copies[0].wait()

    def product(j):
        total = jnp.zeros((rows, cols), F32)
        for i in range(PARTS):
            copies[1 + j * PARTS + i].wait()
            at = slice(i * step, (i + 1) * step)
            total = total + dot_nn(x_ref[:, at], w_ref[j, at, :])
        return total

    pre = product(0)
    query_ref[...] = silu(pre).astype(BF)
    pack_ref[:, 2 * cols : 3 * cols] = silu_grad(pre).astype(BF)
    up = product(1)
    up_ref[...] = up
    pack_ref[:, cols : 2 * cols] = up.astype(BF)
    for c in copies[1 + 2 * PARTS :]:
        c.wait()
    lane = lax.broadcasted_iota(jnp.int32, (rows, IDX_LANES), 1)
    idx = jnp.where(lane == 0, column(owner_ref), column(row_ref))
    pack_ref[:, 3 * cols :] = idx.astype(BF)


def user_of(pos, counts_ref):
    user = jnp.zeros_like(pos)
    end = jnp.int32(0)
    for u in range(counts_ref.shape[0]):
        end = end + counts_ref[u]
        user = user + (pos >= end).astype(jnp.int32)
    return user


def keep_mask(slots, rows, width, first_key, me, counts_ref, lens_ref, live):
    cand = jnp.concatenate(
        [
            lax.broadcasted_iota(jnp.int32, (rows, 1), 0) + (me ^ m) * rows
            for m in range(slots)
        ],
        axis=0,
    )
    key = lax.broadcasted_iota(jnp.int32, (1, width), 1) + first_key
    key_user = jnp.where(live > 0, user_of(key, lens_ref), -1)
    return user_of(cand, counts_ref) == key_user


def diagonal(ref, first, heads):
    parts = [ref[:, (first + h) * HD : (first + h + 1) * HD] for h in range(heads)]
    none = jnp.zeros_like(parts[0])
    return jnp.concatenate(
        [
            jnp.concatenate([parts[h] if h == g else none for g in range(heads)], axis=1)
            for h in range(heads)
        ],
        axis=0,
    )


def chunk_mask(slots, rows, k, width, together, me, counts_ref, lens_ref, live_ref, keys):
    live = live_ref[:, k * width : (k + 1) * width]
    first = me * keys + k * width
    keep = keep_mask(slots, rows, width, first, me, counts_ref, lens_ref, live)
    return jnp.concatenate([keep] * together, axis=0)


def forward_kernel(
    slots, together, width, me_ref, counts_ref, lens_ref, live_ref, kv_ref, *refs
):
    got_refs = refs[:slots]
    sum_ref, low_ref, query_ref = refs[slots : slots + 3]
    half_refs = refs[slots + 3 :]
    cands, cols = sum_ref.shape
    rows = cands // slots
    keys = kv_ref.shape[1]
    me = me_ref[0]
    for m in range(slots):
        query_ref[m * rows : (m + 1) * rows, :] = got_refs[m][...]
    for p in range(0, cols // HD, together):
        at = slice(p * HD, (p + together) * HD)
        query = diagonal(query_ref, p, together)
        total = jnp.zeros((together * cands, together * HD), F32)
        for k in range(keys // width):
            ks = slice(k * width, (k + 1) * width)
            keep = chunk_mask(
                slots, rows, k, width, together, me, counts_ref, lens_ref, live_ref, keys
            )
            half = dot_nt(query, kv_ref[0, ks, at]) * (0.5 * SCALE)
            att = jnp.where(keep, half * jnp.tanh(half) + half, 0.0).astype(BF)
            total = total + dot_nn(att, kv_ref[1, ks, at])
        for h in range(together):
            part = total[h * cands : (h + 1) * cands, h * HD : (h + 1) * HD]
            hs = slice((p + h) * HD, (p + h + 1) * HD)
            sum_ref[:, hs] = part
            low_ref[:, hs] = part.astype(BF)
            for i, ref in enumerate(half_refs):
                size = ref.shape[0]
                ref[:, hs] = part[i * size : (i + 1) * size, :].astype(BF)


def slope_kernel(
    slots, together, width, me_ref, counts_ref, lens_ref, live_ref, kv_ref, query_ref, out_ref
):
    cands, cols = query_ref.shape
    keys = kv_ref.shape[1]
    me = me_ref[0]
    for p in range(0, cols // HD, together):
        at = slice(p * HD, (p + together) * HD)
        query = diagonal(query_ref, p, together)
        for k in range(keys // width):
            ks = slice(k * width, (k + 1) * width)
            keep = chunk_mask(
                slots, cands // slots, k, width, together, me, counts_ref, lens_ref, live_ref, keys
            )
            half = dot_nt(query, kv_ref[0, ks, at]) * (0.5 * SCALE)
            t = jnp.tanh(half)
            slope = 1.0 + t + half * (1.0 - t * t)
            out_ref[p * cands : (p + together) * cands, ks] = jnp.where(keep, slope, 0.0).astype(BF)


def backward_kernel(pieces, slots, together, width, me_ref, gain_ref, up_ref, sum_ref, kv_ref, slope_ref, *refs):
    got, pack_refs = refs[: len(refs) - 2 * slots - 5], refs[len(refs) - 2 * slots - 5 :][:slots]
    refs = refs[len(refs) - slots - 5 :]
    att_ref, upt_ref = refs[:2]
    tile_refs = refs[2 : 2 + slots]
    acc_ref, grad_ref, ug_ref = refs[2 + slots :]
    rows, cols = up_ref.shape
    cands = rows * slots
    keys = kv_ref.shape[1]
    me = me_ref[0]
    packs = [r.at[:, pl.ds(r.shape[1] - 3 * cols - IDX_LANES, 3 * cols + IDX_LANES)] for r in pack_refs]

    for s in range(slots):
        block = slice(s * rows, (s + 1) * rows)
        total = sum_ref[block, :]
        for m in range(1, len(pieces) + 1):
            other = s ^ m
            ref = got[sum(pieces[: m - 1]) + other * pieces[m - 1] // slots]
            start = other * rows % ref.shape[0]
            total = total + ref[start : start + rows, :].astype(F32)
        for h in range(cols // HD):
            at = slice(h * HD, (h + 1) * HD)
            part = total[:, at]
            inv = lax.rsqrt(jnp.mean(part * part, axis=-1, keepdims=True) + NORM_EPS)
            normed = part * inv
            gain = gain_ref[:, at].astype(F32)
            cot = packs[s][:, at].astype(F32)
            if s == 0:
                up = up_ref[:, at]
            else:
                up = packs[s][:, cols + h * HD : cols + (h + 1) * HD].astype(F32)
            gate = silu(up)
            if s == 0:
                att_ref[:, at] = (normed * gain * gate).astype(BF)
            ug_ref[block, at] = (cot * normed * gain * silu_grad(up)).astype(BF)
            ngr = cot * gate * gain
            mean = jnp.mean(ngr * normed, axis=-1, keepdims=True)
            grad_ref[block, at] = (inv * (ngr - normed * mean)).astype(BF)

    for p in range(0, cols // HD, together):
        at = slice(p * HD, (p + together) * HD)
        grad = diagonal(grad_ref, p, together)
        total = jnp.zeros((together * cands, together * HD), F32)
        for k in range(keys // width):
            ks = slice(k * width, (k + 1) * width)
            along = dot_nt(grad, kv_ref[1, ks, at])
            slope = slope_ref[p * cands : (p + together) * cands, ks].astype(F32)
            total = total + dot_nn((slope * along).astype(BF), kv_ref[0, ks, at])
        for h in range(together):
            hs = slice((p + h) * HD, (p + h + 1) * HD)
            acc_ref[:, hs] = total[h * cands : (h + 1) * cands, h * HD : (h + 1) * HD]

    pre_slope = jnp.concatenate([r[:, 2 * cols : 3 * cols] for r in packs], axis=0).astype(F32)
    high, low = split(acc_ref[...] * (0.5 * SCALE) * pre_slope)
    idx = jnp.concatenate([r[:, 3 * cols :] for r in packs], axis=0).astype(F32)
    own, row = idx[:, :1], idx[:, 1:2]
    at_row = lax.broadcasted_iota(jnp.int32, (cands, ITEMS_DEV), 1).astype(F32)
    here = row == at_row
    for m in range(slots):
        mine = own == (me ^ m).astype(F32)
        pick = jnp.where(here & mine, 1.0, 0.0).astype(BF)
        tile_refs[m][...] = (dot_tn(pick, high) + dot_tn(pick, low)).astype(tile_refs[m].dtype)
        if m == 0:
            upt_ref[...] = dot_tn(pick, ug_ref[...])


def weight_kernel(slots, terms, me_ref, w_ref, upt_ref, *refs):
    term_refs, out_refs = refs[:terms], refs[terms:]
    items = upt_ref.shape[0]
    height = out_refs[0].shape[1]
    total = term_refs[0][...]
    for r in term_refs[1:]:
        total = total + r[...].astype(F32)
    table = jnp.concatenate(split(total), axis=0)
    ups = jnp.concatenate(split(upt_ref[...]), axis=0)
    for m in range(slots):
        at = pl.ds(pl.multiple_of((me_ref[0] ^ m) * height, height), height)
        part = dot_nt(table, w_ref[0, at, :]) + dot_nt(ups, w_ref[1, at, :])
        out_refs[m][...] = (part[:items, :] + part[items:, :]).astype(out_refs[m].dtype)


def whole_body(
    cand_feat,
    cand_counts,
    proj_weight,
    norm_gain,
    hist_kv,
    hist_lens,
    hist_mask,
    out_cot,
    owner,
    item_row,
):
    rows, depth = cand_feat.shape
    slots = lax.axis_size("blk")
    wide = lax.axis_size("heads")
    cols = proj_weight.shape[2]
    heads = cols // HD
    cands = rows * slots
    keys = hist_kv.shape[1]
    me = lax.axis_index("blk").astype(jnp.int32).reshape(1)
    head_me = lax.axis_index("heads").astype(jnp.int32).reshape(1)
    live = hist_mask.reshape(1, keys)
    width = min(512, keys)

    together = 2 if heads % 2 == 0 else 1
    pack_cols = 3 * cols + IDX_LANES
    query, pack, up = pl.pallas_call(
        project_kernel,
        in_specs=[pl.BlockSpec(memory_space=HBM)] * 5,
        out_specs=[vmem_spec()] * 3,
        out_shape=[
            pltpu.VMEM((rows, cols), BF),
            pltpu.VMEM((rows, pack_cols), BF),
            pltpu.VMEM((rows, cols), F32),
        ],
        scratch_shapes=[
            pltpu.VMEM((rows, depth), BF),
            pltpu.VMEM((2, depth, cols), BF),
            pltpu.VMEM((1, rows), jnp.int32),
            pltpu.VMEM((1, rows), jnp.int32),
            pltpu.SemaphoreType.DMA((2 * PARTS + 4,)),
        ],
        compiler_params=pltpu.CompilerParams(vmem_limit_bytes=GRANT),
        name="project",
    )(
        far(cand_feat),
        far(proj_weight),
        far(out_cot),
        far(owner.reshape(1, rows)),
        far(item_row.reshape(1, rows)),
    )
    if slots == 4:
        query_slots = gather_slots(query, "blk")
        second = send(pack, "blk", 2)
        pack_slots = [pack, send(pack, "blk", 1), second]
        pack_slots.append(send(second, "blk", 1))
    else:
        query_slots = gather_slots(query, "blk")
        pack_slots = gather_slots(pack, "blk")

    hist_kv = load(hist_kv)
    weight = load(proj_weight)

    every = (cands, cols)
    ranges = [me, cand_counts, hist_lens]
    outs = call(
        functools.partial(forward_kernel, slots, together, width),
        ranges,
        [live, hist_kv, *query_slots],
        [(every, F32), (every, BF), (every, BF)] + [((cands // 2, cols), BF)] * (2 * (slots == 4)),
    )
    sums, low, queries = outs[:3]
    if slots == 4:
        ahead, behind = outs[3:]
        second = [send(ahead, "blk", 2), send(behind, "blk", 2)]
        third = [send(ahead, "blk", 3), send(second[1], "blk", 1)]
        got = [[send(low, "blk", 1)], second, third]
    elif slots <= DIRECT:
        got = [[send(low, "blk", m)] for m in range(1, slots)]
    else:
        order = slot_order("blk")
        whole = lax.psum(sums.reshape(slots, rows, cols)[order], "blk")
        sums, got = whole[order].reshape(cands, cols), []

    slope = call(
        functools.partial(slope_kernel, slots, together, width),
        ranges,
        [live, hist_kv, queries],
        [((heads * cands, keys), BF)],
    )[0]

    tile = (ITEMS_DEV, cols)
    outs = call(
        functools.partial(backward_kernel, [len(g) for g in got], slots, together, width),
        [me],
        [norm_gain.reshape(1, cols), up, sums, hist_kv, slope, *sum(got, []), *pack_slots],
        [((rows, cols), BF), (tile, F32), (tile, F32)] + [(tile, BF)] * (slots - 1),
        [(every, F32), (every, BF), (every, BF)],
    )
    attended, up_table = outs[:2]
    terms = scatter_slots(list(outs[2:]), "blk")

    end = (ITEMS_DEV, depth // wide)
    parts = call(
        functools.partial(weight_kernel, wide, len(terms)),
        [head_me],
        [weight, up_table, *terms],
        [(end, F32)] + [(end, BF)] * (wide - 1),
    )
    ends = scatter_slots(list(parts), "heads")
    item_grad = ends[0]
    for e in ends[1:]:
        item_grad = item_grad + e.astype(F32)
    return (attended, item_grad)


def solution(mesh):
    return jax.shard_map(
        whole_body,
        mesh=mesh,
        in_specs=(
            P(("groups", "blk"), None),
            P("groups"),
            P(None, None, "heads"),
            P("heads"),
            P(None, ("groups", "blk"), "heads"),
            P("groups"),
            P(("groups", "blk")),
            P(("groups", "blk"), "heads"),
            P(("groups", "blk"), None),
            P(("groups", "blk")),
        ),
        out_specs=(P(("groups", "blk"), "heads"), P(("groups", "blk"), "heads")),
        check_vma=False,
    )
```

```python
import functools

import jax
import jax.numpy as jnp
from jax import lax
from jax.experimental import pallas as pl
from jax.experimental.pallas import tpu as pltpu
from jax.sharding import PartitionSpec as P


HD = 128
ITEMS_DEV = 48
NORM_EPS = 1e-05
SCALE = HD ** (-0.5)
IDX_LANES = 128
DIRECT = 4
GRANT = 24 << 20

BF = jnp.bfloat16
F32 = jnp.float32
VMEM = pltpu.MemorySpace.VMEM
SMEM = pltpu.MemorySpace.SMEM
HBM = pltpu.MemorySpace.HBM


def silu(v):
    half = v * 0.5
    return half * jnp.tanh(half) + half


def silu_grad(v):
    half = v * 0.5
    t = jnp.tanh(half)
    return 0.5 * (1.0 + t + half * (1.0 - t * t))


def dot_nt(a, b):
    return lax.dot_general(a, b, (((1,), (1,)), ((), ())), preferred_element_type=F32)


def dot_nn(a, b):
    return lax.dot_general(a, b, (((1,), (0,)), ((), ())), preferred_element_type=F32)


def dot_tn(a, b):
    return lax.dot_general(a, b, (((0,), (0,)), ((), ())), preferred_element_type=F32)


def vmem_spec():
    return pl.BlockSpec(memory_space=VMEM)


def smem_spec():
    return pl.BlockSpec(memory_space=SMEM)


def near(x):
    return pltpu.with_memory_space_constraint(x, VMEM)


def far(x):
    return pltpu.with_memory_space_constraint(x, HBM)


LOADS = 4
PARTS = 4


def load_kernel(src_ref, dst_ref, sems):
    each = LOADS // 2
    step = src_ref.shape[1] // each
    copies = []
    for i in range(LOADS):
        at = pl.ds(i % each * step, step)
        copies.append(
            pltpu.make_async_copy(src_ref.at[i // each, at], dst_ref.at[i // each, at], sems.at[i])
        )
    for c in copies:
        c.start()
    for c in copies:
        c.wait()


def load(x):
    return pl.pallas_call(
        load_kernel,
        in_specs=[pl.BlockSpec(memory_space=HBM)],
        out_specs=vmem_spec(),
        out_shape=pltpu.VMEM(x.shape, x.dtype),
        scratch_shapes=[pltpu.SemaphoreType.DMA((LOADS,))],
        compiler_params=pltpu.CompilerParams(vmem_limit_bytes=GRANT),
    )(far(x))


def call(kernel, scalars, arrays, outs, scratch=()):
    return pl.pallas_call(
        kernel,
        in_specs=[smem_spec()] * len(scalars) + [vmem_spec()] * len(arrays),
        out_specs=[vmem_spec()] * len(outs),
        out_shape=[pltpu.VMEM(shape, kind) for shape, kind in outs],
        scratch_shapes=[pltpu.VMEM(shape, kind) for shape, kind in scratch],
        compiler_params=pltpu.CompilerParams(vmem_limit_bytes=GRANT),
    )(*scalars, *[near(x) for x in arrays])


def slot_order(axis):
    return lax.axis_index(axis) ^ jnp.arange(lax.axis_size(axis), dtype=jnp.int32)


def send(x, axis, m):
    return lax.ppermute(x, axis, [(j, j ^ m) for j in range(lax.axis_size(axis))])


def gather_slots(x, axis):
    n = lax.axis_size(axis)
    if n <= DIRECT:
        return [x] + [send(x, axis, m) for m in range(1, n)]
    whole = lax.all_gather(x, axis)[slot_order(axis)]
    return [whole[m] for m in range(n)]


def scatter_slots(tiles, axis):
    n = lax.axis_size(axis)
    if n <= DIRECT:
        return [tiles[0]] + [send(tiles[m], axis, m) for m in range(1, n)]
    stacked = jnp.stack([t.astype(F32) for t in tiles])[slot_order(axis)]
    return [lax.psum_scatter(stacked, axis, scatter_dimension=0, tiled=False)]


def split(v):
    high = v.astype(BF)
    return high, (v - high.astype(F32)).astype(BF)


def column(line_ref):
    n = line_ref.shape[1]
    same = lax.broadcasted_iota(jnp.int32, (n, n), 0) == lax.broadcasted_iota(jnp.int32, (n, n), 1)
    return jnp.sum(jnp.where(same, line_ref[...], 0).astype(F32), axis=1, keepdims=True)


def project_kernel(
    x_hbm, w_hbm, cot_hbm, owner_hbm, row_hbm, query_ref, pack_ref, up_ref,
    x_ref, w_ref, owner_ref, row_ref, sems,
):
    rows, cols = up_ref.shape
    depth = x_ref.shape[1]
    step = depth // PARTS
    copies = []

    def start(src, dst):
        copies.append(pltpu.make_async_copy(src, dst, sems.at[len(copies)]))
        copies[-1].start()

    start(x_hbm, x_ref)
    for j in range(2):
        for i in range(PARTS):
            at = pl.ds(i * step, step)
            start(w_hbm.at[j, at], w_ref.at[j, at])
    start(cot_hbm, pack_ref.at[:, pl.ds(0, cols)])
    start(owner_hbm, owner_ref)
    start(row_hbm, row_ref)
    copies[0].wait()

    def product(j):
        total = jnp.zeros((rows, cols), F32)
        for i in range(PARTS):
            copies[1 + j * PARTS + i].wait()
            at = slice(i * step, (i + 1) * step)
            total = total + dot_nn(x_ref[:, at], w_ref[j, at, :])
        return total

    pre = product(0)
    query_ref[...] = silu(pre).astype(BF)
    pack_ref[:, 2 * cols : 3 * cols] = silu_grad(pre).astype(BF)
    up = product(1)
    up_ref[...] = up
    pack_ref[:, cols : 2 * cols] = up.astype(BF)
    for c in copies[1 + 2 * PARTS :]:
        c.wait()
    lane = lax.broadcasted_iota(jnp.int32, (rows, IDX_LANES), 1)
    idx = jnp.where(lane == 0, column(owner_ref), column(row_ref))
    pack_ref[:, 3 * cols :] = idx.astype(BF)


def user_of(pos, counts_ref):
    user = jnp.zeros_like(pos)
    end = jnp.int32(0)
    for u in range(counts_ref.shape[0]):
        end = end + counts_ref[u]
        user = user + (pos >= end).astype(jnp.int32)
    return user


def keep_mask(slots, rows, width, first_key, me, counts_ref, lens_ref, live):
    cand = jnp.concatenate(
        [
            lax.broadcasted_iota(jnp.int32, (rows, 1), 0) + (me ^ m) * rows
            for m in range(slots)
        ],
        axis=0,
    )
    key = lax.broadcasted_iota(jnp.int32, (1, width), 1) + first_key
    key_user = jnp.where(live > 0, user_of(key, lens_ref), -1)
    return user_of(cand, counts_ref) == key_user


def diagonal(ref, first, heads):
    parts = [ref[:, (first + h) * HD : (first + h + 1) * HD] for h in range(heads)]
    none = jnp.zeros_like(parts[0])
    return jnp.concatenate(
        [
            jnp.concatenate([parts[h] if h == g else none for g in range(heads)], axis=1)
            for h in range(heads)
        ],
        axis=0,
    )


def chunk_mask(slots, rows, k, width, together, me, counts_ref, lens_ref, live_ref, keys):
    live = live_ref[:, k * width : (k + 1) * width]
    first = me * keys + k * width
    keep = keep_mask(slots, rows, width, first, me, counts_ref, lens_ref, live)
    return jnp.concatenate([keep] * together, axis=0)


def forward_kernel(
    slots, together, width, me_ref, counts_ref, lens_ref, live_ref, kv_ref, *refs
):
    got_refs = refs[:slots]
    sum_ref, low_ref, query_ref = refs[slots : slots + 3]
    half_refs = refs[slots + 3 :]
    cands, cols = sum_ref.shape
    rows = cands // slots
    keys = kv_ref.shape[1]
    me = me_ref[0]
    for m in range(slots):
        query_ref[m * rows : (m + 1) * rows, :] = got_refs[m][...]
    for p in range(0, cols // HD, together):
        at = slice(p * HD, (p + together) * HD)
        query = diagonal(query_ref, p, together)
        total = jnp.zeros((together * cands, together * HD), F32)
        for k in range(keys // width):
            ks = slice(k * width, (k + 1) * width)
            keep = chunk_mask(
                slots, rows, k, width, together, me, counts_ref, lens_ref, live_ref, keys
            )
            half = dot_nt(query, kv_ref[0, ks, at]) * (0.5 * SCALE)
            att = jnp.where(keep, half * jnp.tanh(half) + half, 0.0).astype(BF)
            total = total + dot_nn(att, kv_ref[1, ks, at])
        for h in range(together):
            part = total[h * cands : (h + 1) * cands, h * HD : (h + 1) * HD]
            hs = slice((p + h) * HD, (p + h + 1) * HD)
            sum_ref[:, hs] = part
            low_ref[:, hs] = part.astype(BF)
            for i, ref in enumerate(half_refs):
                size = ref.shape[0]
                ref[:, hs] = part[i * size : (i + 1) * size, :].astype(BF)


def slope_kernel(
    slots, together, width, me_ref, counts_ref, lens_ref, live_ref, kv_ref, query_ref, out_ref
):
    cands, cols = query_ref.shape
    keys = kv_ref.shape[1]
    me = me_ref[0]
    for p in range(0, cols // HD, together):
        at = slice(p * HD, (p + together) * HD)
        query = diagonal(query_ref, p, together)
        for k in range(keys // width):
            ks = slice(k * width, (k + 1) * width)
            keep = chunk_mask(
                slots, cands // slots, k, width, together, me, counts_ref, lens_ref, live_ref, keys
            )
            half = dot_nt(query, kv_ref[0, ks, at]) * (0.5 * SCALE)
            t = jnp.tanh(half)
            slope = 1.0 + t + half * (1.0 - t * t)
            out_ref[p * cands : (p + together) * cands, ks] = jnp.where(keep, slope, 0.0).astype(BF)


def prepare_kernel(slots, me_ref, gain_ref, up_ref, *refs):
    pack_refs = refs[:slots]
    grad_ref, up_grad_ref, pre_ref, gate_ref = refs[slots : slots + 4]
    pick_refs = refs[slots + 4 :]
    rows, cols = up_ref.shape
    me = me_ref[0]
    gain = gain_ref[...].astype(F32)
    for s in range(slots):
        block = slice(s * rows, (s + 1) * rows)
        pack = pack_refs[s]
        scaled = pack[:, :cols].astype(F32) * gain
        up = up_ref[...] if s == 0 else pack[:, cols : 2 * cols].astype(F32)
        gate = silu(up)
        if s == 0:
            gate_ref[...] = gate * gain
        grad_ref[block, :] = scaled * gate
        up_grad_ref[block, :] = scaled * silu_grad(up)
        pre_ref[block, :] = pack[:, 2 * cols : 3 * cols].astype(F32) * (0.5 * SCALE)
    idx = jnp.concatenate([r[:, 3 * cols :] for r in pack_refs], axis=0).astype(F32)
    own, row = idx[:, :1], idx[:, 1:2]
    at_row = lax.broadcasted_iota(jnp.int32, (rows * slots, ITEMS_DEV), 1).astype(F32)
    here = row == at_row
    for m in range(slots):
        mine = own == (me ^ m).astype(F32)
        pick_refs[m][...] = jnp.where(here & mine, 1.0, 0.0).astype(BF)


def backward_kernel(pieces, slots, together, width, *refs):
    refs = list(refs)
    ngr_ref, upc_ref, pre_ref, gate_ref, sum_ref, kv_ref, slope_ref = refs[:7]
    pick_refs = refs[7 : 7 + slots]
    got = refs[7 + slots : 7 + slots + sum(pieces)]
    att_ref, upt_ref, *tile_refs = refs[7 + slots + sum(pieces) : -3]
    acc_ref, grad_ref, ug_ref = refs[-3:]
    rows, cols = att_ref.shape
    cands = rows * slots
    keys = kv_ref.shape[1]

    for s in range(slots):
        block = slice(s * rows, (s + 1) * rows)
        total = sum_ref[block, :]
        for m in range(1, len(pieces) + 1):
            other = s ^ m
            ref = got[sum(pieces[: m - 1]) + other * pieces[m - 1] // slots]
            start = other * rows % ref.shape[0]
            total = total + ref[start : start + rows, :].astype(F32)
        for h in range(cols // HD):
            at = slice(h * HD, (h + 1) * HD)
            part = total[:, at]
            inv = lax.rsqrt(jnp.mean(part * part, axis=-1, keepdims=True) + NORM_EPS)
            normed = part * inv
            if s == 0:
                att_ref[:, at] = (normed * gate_ref[:, at]).astype(BF)
            ug_ref[block, at] = (normed * upc_ref[block, at]).astype(BF)
            ngr = ngr_ref[block, at]
            mean = jnp.mean(ngr * normed, axis=-1, keepdims=True)
            grad_ref[block, at] = (inv * (ngr - normed * mean)).astype(BF)

    for p in range(0, cols // HD, together):
        at = slice(p * HD, (p + together) * HD)
        grad = diagonal(grad_ref, p, together)
        total = jnp.zeros((together * cands, together * HD), F32)
        for k in range(keys // width):
            ks = slice(k * width, (k + 1) * width)
            along = dot_nt(grad, kv_ref[1, ks, at])
            slope = slope_ref[p * cands : (p + together) * cands, ks].astype(F32)
            total = total + dot_nn((slope * along).astype(BF), kv_ref[0, ks, at])
        for h in range(together):
            hs = slice((p + h) * HD, (p + h + 1) * HD)
            acc_ref[:, hs] = total[h * cands : (h + 1) * cands, h * HD : (h + 1) * HD]

    high, low = split(acc_ref[...] * pre_ref[...])
    for m in range(slots):
        pick = pick_refs[m][...]
        tile_refs[m][...] = (dot_tn(pick, high) + dot_tn(pick, low)).astype(tile_refs[m].dtype)
        if m == 0:
            upt_ref[...] = dot_tn(pick, ug_ref[...])


def weight_kernel(order, terms, me_ref, w_ref, *refs):
    term_refs, out_refs = refs[:terms], refs[terms:]
    if terms > 2:
        upt_ref, table_ref, ups_ref = term_refs[0], out_refs[-2], out_refs[-1]
        total = term_refs[1][...]
        for r in term_refs[2:]:
            total = total + r[...].astype(F32)
        table_ref[...] = jnp.concatenate(split(total), axis=0)
        ups_ref[...] = jnp.concatenate(split(upt_ref[...]), axis=0)
    else:
        table_ref, ups_ref = term_refs
    items, height = out_refs[0].shape
    table, ups = table_ref[...], ups_ref[...]
    for m, out_ref in zip(order, out_refs):
        at = pl.ds(pl.multiple_of((me_ref[0] ^ m) * height, height), height)
        part = dot_nt(table, w_ref[0, at, :]) + dot_nt(ups, w_ref[1, at, :])
        out_ref[...] = (part[:items, :] + part[items:, :]).astype(out_ref.dtype)


def whole_body(
    cand_feat,
    cand_counts,
    proj_weight,
    norm_gain,
    hist_kv,
    hist_lens,
    hist_mask,
    out_cot,
    owner,
    item_row,
):
    rows, depth = cand_feat.shape
    slots = lax.axis_size("blk")
    wide = lax.axis_size("heads")
    cols = proj_weight.shape[2]
    heads = cols // HD
    cands = rows * slots
    keys = hist_kv.shape[1]
    me = lax.axis_index("blk").astype(jnp.int32).reshape(1)
    head_me = lax.axis_index("heads").astype(jnp.int32).reshape(1)
    live = hist_mask.reshape(1, keys)
    width = keys if cands <= 256 else min(512, keys)
    narrow = min(128, keys)

    together = 2 if heads % 2 == 0 else 1
    pack_cols = 3 * cols + IDX_LANES
    query, pack, up = pl.pallas_call(
        project_kernel,
        in_specs=[pl.BlockSpec(memory_space=HBM)] * 5,
        out_specs=[vmem_spec()] * 3,
        out_shape=[
            pltpu.VMEM((rows, cols), BF),
            pltpu.VMEM((rows, pack_cols), BF),
            pltpu.VMEM((rows, cols), F32),
        ],
        scratch_shapes=[
            pltpu.VMEM((rows, depth), BF),
            pltpu.VMEM((2, depth, cols), BF),
            pltpu.VMEM((1, rows), jnp.int32),
            pltpu.VMEM((1, rows), jnp.int32),
            pltpu.SemaphoreType.DMA((2 * PARTS + 4,)),
        ],
        compiler_params=pltpu.CompilerParams(vmem_limit_bytes=GRANT),
        name="project",
    )(
        far(cand_feat),
        far(proj_weight),
        far(out_cot),
        far(owner.reshape(1, rows)),
        far(item_row.reshape(1, rows)),
    )
    if slots == 4:
        query_slots = gather_slots(query, "blk")
        second = send(pack, "blk", 2)
        pack_slots = [pack, send(pack, "blk", 1), second]
        pack_slots.append(send(second, "blk", 1))
    else:
        query_slots = gather_slots(query, "blk")
        pack_slots = gather_slots(pack, "blk")

    hist_kv = load(hist_kv)
    weight = load(proj_weight)

    every = (cands, cols)
    ranges = [me, cand_counts, hist_lens]
    outs = call(
        functools.partial(forward_kernel, slots, together, width),
        ranges,
        [live, hist_kv, *query_slots],
        [(every, F32), (every, BF), (every, BF)] + [((cands // 2, cols), BF)] * (2 * (slots == 4)),
    )
    sums, low, queries = outs[:3]
    if slots == 4:
        ahead, behind = outs[3:]
        second = [send(ahead, "blk", 2), send(behind, "blk", 2)]
        third = [send(ahead, "blk", 3), send(second[1], "blk", 1)]
        got = [[send(low, "blk", 1)], second, third]
    elif slots <= DIRECT:
        got = [[send(low, "blk", m)] for m in range(1, slots)]
    else:
        order = slot_order("blk")
        whole = lax.psum(sums.reshape(slots, rows, cols)[order], "blk")
        sums, got = whole[order].reshape(cands, cols), []

    slope = call(
        functools.partial(slope_kernel, slots, together, width),
        ranges,
        [live, hist_kv, queries],
        [((heads * cands, keys), BF)],
    )[0]

    tile = (ITEMS_DEV, cols)
    ready = call(
        functools.partial(prepare_kernel, slots),
        [me],
        [norm_gain.reshape(1, cols), up, *pack_slots],
        [(every, F32)] * 3 + [((rows, cols), F32)] + [((cands, ITEMS_DEV), BF)] * slots,
    )
    outs = call(
        functools.partial(backward_kernel, [len(g) for g in got], slots, together, narrow),
        [],
        [*ready[:4], sums, hist_kv, slope, *ready[4:], *sum(got, [])],
        [((rows, cols), BF), (tile, F32), (tile, F32)] + [(tile, BF)] * (slots - 1),
        [(every, F32), (every, BF), (every, BF)],
    )
    attended, up_table = outs[:2]
    terms = scatter_slots(list(outs[2:]), "blk")

    end = (ITEMS_DEV, depth // wide)
    order = list(range(wide))[::-1]
    ahead, behind = order[: wide // 2], order[wide // 2 :]
    kind = [F32] + [BF] * (wide - 1)
    pair = ((2 * ITEMS_DEV, cols), BF)
    up_terms = [up_table, *terms] if len(terms) > 1 else [up_table, *terms, jnp.zeros(tile, BF)]
    parts = call(
        functools.partial(weight_kernel, ahead, len(up_terms)),
        [head_me],
        [weight, *up_terms],
        [(end, kind[m]) for m in ahead] + [pair, pair],
    )
    halves = list(parts[-2:])
    parts = list(parts[:-2]) + list(
        call(
            functools.partial(weight_kernel, behind, 2),
            [head_me],
            [weight, *halves],
            [(end, kind[m]) for m in behind],
        )
    )
    ends = scatter_slots(parts[::-1], "heads")
    item_grad = ends[0]
    for e in ends[1:]:
        item_grad = item_grad + e.astype(F32)
    return (attended, item_grad)


def solution(mesh):
    return jax.shard_map(
        whole_body,
        mesh=mesh,
        in_specs=(
            P(("groups", "blk"), None),
            P("groups"),
            P(None, None, "heads"),
            P("heads"),
            P(None, ("groups", "blk"), "heads"),
            P("groups"),
            P(("groups", "blk")),
            P(("groups", "blk"), "heads"),
            P(("groups", "blk"), None),
            P(("groups", "blk")),
        ),
        out_specs=(P(("groups", "blk"), "heads"), P(("groups", "blk"), "heads")),
        check_vma=False,
    )
```
